256 devices in a mesh: rows: 256 (over y, z, x, core).
Axes of the slice: x: 4, y: 4, z: 8, core: 2. Of those that a mesh axis runs over, the one named last changes fastest.
Arguments:
- right_side: float32 [4194304], P('rows'), may hold values from -24 to 24
- diag_shift: float32 [4194304], P('rows'), may hold values from 0.05 to 0.5
- dictionary: float32 [128, 128, 128], replicated, may hold values from -16.5 to 16.5, as said below
- diag_ids: int32 [32768], P('rows'), may hold values from 0 to 127
- diag_gain: float32 [32768], P('rows'), may hold values from 0.3 to 1.5
- cycle_ids: int32 [32768, 2], P('rows'), may hold values from 0 to 127, as said below
- cycle_weights: float32 [32768, 2], P('rows'), may hold values from 0.3 to 1.5, as said below
- link_rows: int32 [256, 5, 64], P('rows'), may hold values from 0 to 127, as said below
- link_ids: int32 [256, 5, 64], P('rows'), may hold values from 0 to 127, as said below
- link_weights: float32 [256, 5, 64], P('rows'), may hold values from 0.3 to 1.5, as said below
Outputs:
- solution_field: float32 [4194304], P('rows')
- residual: float32 [4194304], P('rows')
The draws below stay inside these ranges and needn't reach their ends.
Inputs may be any that keep to these rules, and one draw needn't show every extreme that they name: `dictionary`: every block is symmetric positive definite. cycle_ids[i,1] equals cycle_ids[(i+1) mod 32768,0]. cycle_weights[i,1] equals cycle_weights[(i+1) mod 32768,0]. `link_rows`: for each device and level the 64 entries are distinct. `link_ids`: devices d and d XOR 2^b at level m (b = log2 of the number of devices - 1 - m) hold the same entries in the same order. `link_weights`: devices d and d XOR 2^b at level m (b = log2 of the number of devices - 1 - m) hold the same entries in the same order.
All inputs are finite; a program needn't handle non-finite values.
Results may differ from the reference program's by a relative error of at most 0.0003.
Values sent between devices are 32-bit elements; how exact they have to be, the bound alone decides.
A program may use at most 128 MiB of HBM per device.

```python
import math
import jax
import jax.numpy as jnp
from jax import lax

BS = 128
DICT = 128
NB_DEV = 128
ITERS = 4
LEVELS = 5
HALF = 64
BLOCKS = 32768


def draw_right_side(key, part):
    length_all = BLOCKS * BS
    rising = 1.0 + 2.0 * jnp.arange(length_all, dtype=jnp.float32) / length_all
    normal_part = jnp.clip(jax.random.normal(key, (length_all,), jnp.float32), -4.0, 4.0)
    return 2.0 * rising * normal_part


def draw_dictionary(key, part):
    factor = jnp.clip(jax.random.normal(jax.random.fold_in(key, 13), (DICT, BS, BS), jnp.float32), -4.0, 4.0)
    gram_blocks = jnp.einsum('kij,klj->kil', factor, factor, precision=jax.lax.Precision.HIGHEST) / BS
    return gram_blocks + 0.5 * jnp.eye(BS, dtype=jnp.float32)


def cycle_pair(values):
    return jnp.stack([jnp.roll(values, 1), values], axis=1)


def draw_cycle_ids(key, part):
    drawn = jax.random.randint(jax.random.fold_in(key, 21), (BLOCKS,), 0, DICT, jnp.int32)
    return cycle_pair(drawn)


def weight_values(key, shape):
    return jnp.exp(jax.random.uniform(key, shape, jnp.float32, math.log(0.3), math.log(1.5)))


def draw_cycle_weights(key, part):
    return cycle_pair(weight_values(jax.random.fold_in(key, 22), (BLOCKS,)))


def mirror(drawn):
    devices = BLOCKS // NB_DEV
    bit_count = devices.bit_length() - 1
    owners = jnp.arange(devices, dtype=jnp.int32)
    stacked = []
    for level_idx in range(LEVELS):
        partner = jnp.bitwise_xor(owners, jnp.int32(1 << bit_count - 1 - level_idx))
        lowest = jnp.minimum(owners, partner)
        stacked.append(drawn[lowest, level_idx])
    return jnp.stack(stacked, axis=1)


def draw_link_rows(key, part):
    devices = BLOCKS // NB_DEV
    subkeys = jax.random.split(jax.random.fold_in(key, 31), devices * LEVELS)
    orders = jax.vmap(lambda subkey: jax.random.permutation(subkey, NB_DEV))(subkeys)
    return orders[:, :HALF].reshape(devices, LEVELS, HALF).astype(jnp.int32)


def draw_link_ids(key, part):
    devices = BLOCKS // NB_DEV
    drawn = jax.random.randint(jax.random.fold_in(key, 32), (devices, LEVELS, HALF), 0, DICT, jnp.int32)
    return mirror(drawn)


def draw_link_weights(key, part):
    devices = BLOCKS // NB_DEV
    return mirror(weight_values(jax.random.fold_in(key, 33), (devices, LEVELS, HALF)))


def set_ends(entries, key, least, top_value):
    shape = entries.shape
    spot = [jax.random.randint(jax.random.fold_in(key, axis), (), 0, shape[axis]) for axis in range(len(shape))]
    entries = entries.at[tuple(spot)].set(least)
    longest = shape.index(max(shape))
    spot[longest] = (spot[longest] + 1) % shape[longest]
    return entries.at[tuple(spot)].set(top_value)


def block_scale(key, dims, shards, smallest, high):
    def one(axis_at, parts):
        steps = jax.random.uniform(jax.random.fold_in(jax.random.fold_in(key, 6), axis_at), (parts,), jnp.float32, smallest / len(shards), high / len(shards))
        return jnp.repeat(jnp.exp(steps), dims[axis_at] // parts).reshape((-1,) + (1,) * (len(dims) - axis_at - 1))

    level = one(*shards[0])
    for cut in shards[1:]:
        level = level * one(*cut)
    return level


def setup_inputs(seed: int = 0) -> dict:
    key_list = jax.random.split(jax.random.key(seed), 11)
    right_side = draw_right_side(jax.random.fold_in(key_list[10], 71), 0)
    diag_shift = jnp.clip(jnp.exp(math.log(0.5) - 2.3025851 * jax.random.uniform(key_list[1], (BLOCKS * BS,), jnp.float32) ** block_scale(key_list[1], (BLOCKS * BS,), ((0, 256),), -0.2, 0.2)), 0.05, 0.5)
    dictionary = draw_dictionary(jax.random.fold_in(key_list[10], 71), 0)
    diag_ids = set_ends(jax.random.randint(key_list[3], (BLOCKS,), 0, DICT), jax.random.fold_in(key_list[3], 1), 0, DICT - 1).astype(jnp.int32)
    diag_gain = jnp.clip(jnp.exp(math.log(1.5) - 1.60943787 * jax.random.uniform(key_list[4], (BLOCKS,), jnp.float32) ** block_scale(key_list[4], (BLOCKS,), ((0, 256),), -0.2, 0.2)), 0.3, 1.5)
    cycle_ids = draw_cycle_ids(jax.random.fold_in(key_list[10], 71), 0)
    cycle_weights = draw_cycle_weights(jax.random.fold_in(key_list[10], 71), 0)
    link_rows = draw_link_rows(jax.random.fold_in(key_list[10], 71), 0)
    link_ids = draw_link_ids(jax.random.fold_in(key_list[10], 71), 0)
    link_weights = draw_link_weights(jax.random.fold_in(key_list[10], 71), 0)
    return dict(right_side=right_side, diag_shift=diag_shift, dictionary=dictionary, diag_ids=diag_ids, diag_gain=diag_gain, cycle_ids=cycle_ids, cycle_weights=cycle_weights, link_rows=link_rows, link_ids=link_ids, link_weights=link_weights)


def batched(mats, vectors):
    return jnp.einsum('nij,nj->ni', mats, vectors, precision=lax.Precision.HIGHEST)


def apply_operator(vector, diag_shift, dictionary, diag_ids, diag_gain, cycle_ids, cycle_weights, link_rows, link_ids, link_weights):
    devices = BLOCKS // NB_DEV
    bit_count = devices.bit_length() - 1
    flat = vector.reshape(BLOCKS, BS)
    lower_blocks = jnp.roll(flat, 1, axis=0).reshape(devices, NB_DEV, BS)
    upper_blocks = jnp.roll(flat, -1, axis=0).reshape(devices, NB_DEV, BS)
    grouped = flat.reshape(devices, NB_DEV, BS)
    owners = jnp.arange(devices, dtype=jnp.int32)
    differences = []
    for level_idx in range(LEVELS):
        partner = jnp.bitwise_xor(owners, jnp.int32(1 << (bit_count - 1 - level_idx)))
        own_part = grouped[owners[:, None], link_rows[:, level_idx]]
        remote = grouped[partner[:, None], link_rows[partner, level_idx]]
        differences.append(own_part - remote)
    link_diff = jnp.stack(differences, axis=1)

    def one_device(pieces):
        block_vec, below_vec, above_vec, shifts, dids, dgain, rids, rweights, lrows, lids, lweights, ldiff = pieces
        diag_mats = dictionary[dids] * dgain[:, None, None]
        lower_mats = dictionary[rids[:, 0]] * rweights[:, 0, None, None]
        upper_mats = dictionary[rids[:, 1]] * rweights[:, 1, None, None]
        result = shifts * block_vec + batched(diag_mats, block_vec)
        result = result + batched(lower_mats, block_vec - below_vec) + batched(upper_mats, block_vec - above_vec)
        link_mats = dictionary[lids] * lweights[:, :, None, None]
        products = jnp.einsum('lhij,lhj->lhi', link_mats, ldiff, precision=lax.Precision.HIGHEST)
        selector = (lrows[:, :, None] == jnp.arange(NB_DEV, dtype=jnp.int32)).astype(jnp.float32)
        return result + jnp.einsum('lhn,lhi->ni', selector, products, precision=lax.Precision.HIGHEST)

    results = lax.map(one_device, (grouped, lower_blocks, upper_blocks, diag_shift.reshape(devices, NB_DEV, BS),
                                   diag_ids.reshape(devices, NB_DEV), diag_gain.reshape(devices, NB_DEV),
                                   cycle_ids.reshape(devices, NB_DEV, 2), cycle_weights.reshape(devices, NB_DEV, 2),
                                   link_rows, link_ids, link_weights, link_diff))
    return results.reshape(-1)


def reference(right_side, diag_shift, dictionary, diag_ids, diag_gain, cycle_ids, cycle_weights, link_rows, link_ids, link_weights):
    def operate(vector):
        return apply_operator(vector, diag_shift, dictionary, diag_ids, diag_gain, cycle_ids, cycle_weights, link_rows, link_ids, link_weights)

    solution_field = jnp.zeros_like(right_side)
    residual = right_side
    image_vec = operate(residual)
    norm_now = jnp.sum(residual * residual)
    product = jnp.sum(residual * image_vec)
    step_size = norm_now / product
    direction, image_dir = residual, image_vec
    for iteration in range(ITERS):
        solution_field = solution_field + step_size * direction
        residual = residual - step_size * image_dir
        if iteration + 1 < ITERS:
            image_vec = operate(residual)
            norm_next = jnp.sum(residual * residual)
            product = jnp.sum(residual * image_vec)
            beta_ratio = norm_next / norm_now
            step_size = norm_next / (product - beta_ratio * norm_next / step_size)
            direction = residual + beta_ratio * direction
            image_dir = image_vec + beta_ratio * image_dir
            norm_now = norm_next
    return solution_field, residual
```

```python
import functools

import jax
import jax.numpy as jnp
from jax import lax
from jax.experimental import pallas as pl
from jax.experimental.pallas import tpu as pltpu
from jax.sharding import PartitionSpec as P

AXIS = "rows"
MESH = pl.DeviceIdType.MESH
ITERS = 4
BS = 128
NB = 128
HALF = 64
LEVELS = 5
LINKS = LEVELS * HALF
LEVEL_OF = (4, 1, 3, 0, 2)
EDGE0 = NB
LINK0 = 2 * NB
BOUND0 = LINK0 + 3 * NB
TOTAL = BOUND0 + NB
PARTS = 16
F32 = jnp.float32
BF16 = jnp.bfloat16


def level_mask(li):
    q = li // 2
    return 8 * (1 + q + q // 2) * (1 + 7 * (li % 2))


def level_partner(me, li):
    mask = level_mask(li)
    return me + mask - 2 * mask * ((me // mask) % 2)


def split_rows(d):
    high = d.astype(BF16).astype(F32)
    return jnp.concatenate([high, d - high], axis=0).astype(BF16)


def kernel(
    ids, rows, b_ref, shift_ref, dict_ref, wrow_ref, lrow_ref,
    x_ref, r_ref,
    g_ref, stage, wv, st, upad, w_ref, p_ref, s_ref, z_ref, acc_ref, f_ref, ol_ref, scal,
    send, recv, csend, crecv, ar_src, ar_one, ar_mid, ar_two,
    dict_sem, lv_s, lv_r, cy_s, cy_r, a1_s, a1_r, a2_s, a2_r,
):
    me = lax.axis_index(AXIS)
    n = lax.axis_size(AXIS)
    core, xs, zs, ys = me % 2, (me // 2) % 4, (me // 8) % 8, me // 64
    nxt, prv = (me + 1) % n, (me + n - 1) % n

    def one_peer(j):
        return ys * 64 + ((zs + j // 2) % 8) * 8 + xs * 2 + (core + j % 2) % 2

    def two_peer(j):
        return ((ys + j // 4) % 4) * 64 + zs * 8 + ((xs + j % 4) % 4) * 2 + core

    def dict_copy(c):
        part = pl.ds(c * 8, 8)
        return pltpu.make_async_copy(dict_ref.at[part], stage.at[part], dict_sem.at[c])

    @pl.loop(0, 16)
    def _(c):
        dict_copy(c).start()

    barrier = pltpu.get_barrier_semaphore()

    @pl.loop(1, PARTS)
    def _(j):
        pl.semaphore_signal(barrier, inc=1, device_id={AXIS: one_peer(j)}, device_id_type=MESH)
        pl.semaphore_signal(barrier, inc=1, device_id={AXIS: two_peer(j)}, device_id_type=MESH)

    pl.semaphore_signal(barrier, inc=1, device_id={AXIS: nxt}, device_id_type=MESH)
    pl.semaphore_signal(barrier, inc=1, device_id={AXIS: prv}, device_id_type=MESH)

    eye = lax.broadcasted_iota(jnp.int32, (NB, BS), 0) == lax.broadcasted_iota(jnp.int32, (NB, BS), 1)
    for blk in range(6):
        column = jnp.sum(jnp.where(eye, wrow_ref[blk : blk + 1, :], 0.0), axis=1, keepdims=True)
        wv[blk * NB : (blk + 1) * NB, :] = jnp.broadcast_to(column, (NB, BS))
    for blk in range(3):
        cols = slice(blk * BS, (blk + 1) * BS)
        hit = lax.broadcasted_iota(jnp.int32, (NB, BS), 0) == lrow_ref[0:1, cols]
        st[:, cols] = jnp.where(hit, 1.0, 0.0).astype(BF16)
    zeros = jnp.zeros((NB, BS), F32)
    upad[0:8, :] = jnp.zeros((8, BS), F32)
    upad[8 : 8 + NB, :] = b_ref[...]
    x_ref[...] = zeros
    r_ref[...] = b_ref[...]
    p_ref[...] = zeros
    s_ref[...] = zeros
    z_ref[...] = zeros
    ol_ref[LINKS:, :] = jnp.zeros((64, 2 * BS), F32)
    scal[...] = jnp.ones((2, 8, BS), F32)

    @pl.loop(0, 16)
    def _(c):
        dict_copy(c).wait()

        @pl.loop(0, 8)
        def _(i):
            block = stage[c * 8 + i]
            high = block.astype(BF16)
            g_ref[c * 8 + i, :, 0:BS] = high
            g_ref[c * 8 + i, :, BS:] = (block - high.astype(F32)).astype(BF16)

    pl.semaphore_wait(barrier, 2 * (PARTS - 1) + 2)

    sub16 = lax.broadcasted_iota(jnp.int32, (16, BS), 0) % 8

    def products(d, base, count):
        lhs = split_rows(d)
        out = jnp.zeros((16, 2 * BS), F32)
        for j in range(count):
            picked = jnp.where(sub16 == j, lhs, jnp.zeros_like(lhs))
            out = out + jnp.dot(picked, g_ref[ids[base + j]], preferred_element_type=F32)
        return out[:8, :BS] + out[:8, BS:] + out[8:, :BS]

    def level_copy(k, li):
        return pltpu.make_async_remote_copy(
            src_ref=send.at[k, li], dst_ref=recv.at[k, li], send_sem=lv_s.at[k, li], recv_sem=lv_r.at[k, li],
            device_id={AXIS: level_partner(me, li)}, device_id_type=MESH)

    def cycle_copy(k, side):
        return pltpu.make_async_remote_copy(
            src_ref=csend.at[k, side], dst_ref=crecv.at[k, side], send_sem=cy_s.at[k, side],
            recv_sem=cy_r.at[k, side], device_id={AXIS: nxt if side == 0 else prv}, device_id_type=MESH)

    def one_copy(k, j):
        return pltpu.make_async_remote_copy(
            src_ref=ar_src.at[k], dst_ref=ar_one.at[k, j], send_sem=a1_s.at[k, j], recv_sem=a1_r.at[k, j],
            device_id={AXIS: one_peer(j)}, device_id_type=MESH)

    def two_copy(k, j):
        return pltpu.make_async_remote_copy(
            src_ref=ar_mid.at[k], dst_ref=ar_two.at[k, j], send_sem=a2_s.at[k, j], recv_sem=a2_r.at[k, j],
            device_id={AXIS: two_peer(j)}, device_id_type=MESH)

    def reduce_begin(k):
        @pl.loop(1, PARTS)
        def _(j):
            one_copy(k, j).start()

    def reduce_middle(k):
        @pl.loop(1, PARTS)
        def _(j):
            one_copy(k, j).wait()

        ar_one[k, 0] = ar_src[k]
        ar_mid[k] = jnp.sum(ar_one[k], axis=0)

        @pl.loop(1, PARTS)
        def _(j):
            two_copy(k, j).start()

    def reduce_end(k):
        @pl.loop(1, PARTS)
        def _(j):
            two_copy(k, j).wait()

        ar_two[k, 0] = ar_mid[k]
        total = jnp.sum(ar_two[k], axis=0)
        sums = jnp.sum(total, axis=1, keepdims=True)
        norm = jnp.broadcast_to(sums[0:1, :], (8, BS))
        product = jnp.broadcast_to(sums[1:2, :], (8, BS))
        return norm, product

    def coefficients(k, norm, product):
        first = jnp.where(k == 0, 0.0, 1.0).astype(F32)
        beta = first * (norm / scal[0])
        alpha = norm / (product - beta * norm / scal[1])
        scal[0] = norm
        scal[1] = alpha
        return alpha, beta

    def put_sums(k):
        r = r_ref[...]
        ar_src[k, 0:1, :] = jnp.sum(r * r, axis=0, keepdims=True)
        ar_src[k, 1:2, :] = jnp.sum(r * w_ref[...], axis=0, keepdims=True)

    def operate(k):
        @pl.loop(0, LEVELS)
        def _(i):
            li = LEVELS - 1 - i

            @pl.loop(0, HALF // 16)
            def _(h):
                for j in range(16):
                    row = rows[li * HALF + h * 16 + j]
                    send[k, li, pl.ds(h * 16 + j, 1), :] = upad[pl.ds(row + 8, 1), :]

            level_copy(k, li).start()

        csend[k, 0] = upad[7 + NB : 8 + NB, :]
        csend[k, 1] = upad[8:9, :]
        cycle_copy(k, 0).start()
        cycle_copy(k, 1).start()

        def local(t, carry):
            for half in range(4):
                g = pl.multiple_of(t * 32 + half * 8, 8)
                here = upad[pl.ds(g + 8, 8), :]
                before = upad[pl.ds(g + 7, 8), :]
                acc_ref[pl.ds(g, 8), :] = shift_ref[pl.ds(g, 8), :] * here + products(
                    here * wv[pl.ds(g, 8), :], g, 8
                )
                f_ref[pl.ds(g, 8), :] = products((here - before) * wv[pl.ds(EDGE0 + g, 8), :], EDGE0 + g, 8)
            return carry

        lax.fori_loop(0, 4, local, 0)

        @pl.when(k > 0)
        def _():
            reduce_middle(k - 1)

        def level(li, carry):
            level_copy(k, li).wait_recv()
            for h in range(8):
                c = pl.multiple_of(li * HALF + h * 8, 8)
                diff = send[k, li, h * 8 : h * 8 + 8, :] - recv[k, li, h * 8 : h * 8 + 8, :]
                out = products(diff * wv[pl.ds(LINK0 + c, 8), :], LINK0 + c, 8)
                high = out.astype(BF16).astype(F32)
                ol_ref[pl.ds(c, 8), 0:BS] = high
                ol_ref[pl.ds(c, 8), BS:] = out - high
            return carry

        lax.fori_loop(0, LEVELS, level, 0)
        cycle_copy(k, 0).wait()
        cycle_copy(k, 1).wait()
        sub8 = lax.broadcasted_iota(jnp.int32, (8, BS), 0)
        edge = jnp.where(sub8 == 0, upad[8:9, :] - crecv[k, 0], crecv[k, 1] - upad[7 + NB : 8 + NB, :])
        bound = products(edge * wv[BOUND0 : BOUND0 + 8, :], BOUND0, 2)
        f_ref[0:1, :] = bound[0:1, :]
        f_ref[NB : NB + 1, :] = bound[1:2, :]
        spread = jnp.dot(st[...], ol_ref[...].astype(BF16), preferred_element_type=F32)
        acc_ref[...] = acc_ref[...] + (f_ref[0:NB, :] - f_ref[1 : NB + 1, :]) + (spread[:, :BS] + spread[:, BS:])

        @pl.loop(0, LEVELS)
        def _(li):
            level_copy(k, li).wait_send()


    def iteration(k, carry):
        @pl.when(k > 0)
        def _():
            reduce_begin(k - 1)

        operate(k)

        @pl.when(k == 0)
        def _():
            w_ref[...] = acc_ref[...]

        @pl.when(k > 0)
        def _():
            alpha, beta = coefficients(k - 1, *reduce_end(k - 1))
            alpha, beta = jnp.tile(alpha, (16, 1)), jnp.tile(beta, (16, 1))
            p = r_ref[...] + beta * p_ref[...]
            s = w_ref[...] + beta * s_ref[...]
            z = acc_ref[...] + beta * z_ref[...]
            p_ref[...] = p
            s_ref[...] = s
            z_ref[...] = z
            x_ref[...] = x_ref[...] + alpha * p
            r_ref[...] = r_ref[...] - alpha * s
            w_ref[...] = w_ref[...] - alpha * z

        upad[8 : 8 + NB, :] = w_ref[...]
        put_sums(k)
        return carry

    lax.fori_loop(0, ITERS, iteration, 0)
    last = ITERS - 1
    reduce_begin(last)
    reduce_middle(last)
    alpha, beta = coefficients(last, *reduce_end(last))
    alpha, beta = jnp.tile(alpha, (16, 1)), jnp.tile(beta, (16, 1))
    x_ref[...] = x_ref[...] + alpha * (r_ref[...] + beta * p_ref[...])
    r_ref[...] = r_ref[...] - alpha * (w_ref[...] + beta * s_ref[...])


def per_device(
    right_side,
    diag_shift,
    dictionary,
    diag_ids,
    diag_gain,
    cycle_ids,
    cycle_weights,
    link_rows,
    link_ids,
    link_weights,
):

    def reordered(values):
        return jnp.concatenate([values[0, m] for m in LEVEL_OF])

    def table(diag, cycle, link):
        return jnp.concatenate(
            [diag, cycle[:, 0], reordered(link), jnp.zeros((64,), diag.dtype), cycle[0, :1], cycle[-1, 1:],
             jnp.zeros((126,), diag.dtype)])

    ids = table(diag_ids, cycle_ids, link_ids)
    weights = table(diag_gain, cycle_weights, link_weights).reshape(6, BS)
    rows = jnp.concatenate([reordered(link_rows), jnp.full((64,), -1, jnp.int32)])
    vec = (NB, BS)
    smem = pl.BlockSpec(memory_space=pltpu.SMEM)
    vmem = pl.BlockSpec(memory_space=pltpu.VMEM)
    solved, residual = pl.pallas_call(
        kernel,
        out_shape=(jax.ShapeDtypeStruct(vec, F32), jax.ShapeDtypeStruct(vec, F32)),
        in_specs=[smem, smem, vmem, vmem, pl.BlockSpec(memory_space=pl.ANY), vmem, vmem],
        out_specs=(vmem, vmem),
        scratch_shapes=[
            pltpu.VMEM((BS, BS, 2 * BS), BF16),
            pltpu.VMEM((BS, BS, BS), F32),
            pltpu.VMEM((TOTAL, BS), F32),
            pltpu.VMEM((NB, 3 * BS), BF16),
            pltpu.VMEM((NB + 8, BS), F32),
            pltpu.VMEM(vec, F32),
            pltpu.VMEM(vec, F32),
            pltpu.VMEM(vec, F32),
            pltpu.VMEM(vec, F32),
            pltpu.VMEM(vec, F32),
            pltpu.VMEM((NB + 8, BS), F32),
            pltpu.VMEM((3 * BS, 2 * BS), F32),
            pltpu.VMEM((2, 8, BS), F32),
            pltpu.VMEM((ITERS, LEVELS, HALF, BS), F32),
            pltpu.VMEM((ITERS, LEVELS, HALF, BS), F32),
            pltpu.VMEM((ITERS, 2, 1, BS), F32),
            pltpu.VMEM((ITERS, 2, 1, BS), F32),
            pltpu.VMEM((ITERS, 2, BS), F32),
            pltpu.VMEM((ITERS, PARTS, 2, BS), F32),
            pltpu.VMEM((ITERS, 2, BS), F32),
            pltpu.VMEM((ITERS, PARTS, 2, BS), F32),
            pltpu.SemaphoreType.DMA((16,)),
            pltpu.SemaphoreType.DMA((ITERS, LEVELS)),
            pltpu.SemaphoreType.DMA((ITERS, LEVELS)),
            pltpu.SemaphoreType.DMA((ITERS, 2)),
            pltpu.SemaphoreType.DMA((ITERS, 2)),
            pltpu.SemaphoreType.DMA((ITERS, PARTS)),
            pltpu.SemaphoreType.DMA((ITERS, PARTS)),
            pltpu.SemaphoreType.DMA((ITERS, PARTS)),
            pltpu.SemaphoreType.DMA((ITERS, PARTS)),
        ],
        compiler_params=pltpu.CompilerParams(
            collective_id=0, has_side_effects=True, vmem_limit_bytes=40 * 1024 * 1024
        ),
        name="cg",
    )(ids, rows, right_side.reshape(vec), diag_shift.reshape(vec), dictionary, weights, rows.reshape(1, 3 * BS))
    return solved.reshape(-1), residual.reshape(-1)


def solution(mesh):
    placed = (
        P(AXIS),
        P(AXIS),
        P(),
        P(AXIS),
        P(AXIS),
        P(AXIS, None),
        P(AXIS, None),
        P(AXIS, None, None),
        P(AXIS, None, None),
        P(AXIS, None, None),
    )
    return jax.shard_map(
        per_device, mesh=mesh, in_specs=placed, out_specs=(P(AXIS), P(AXIS)), check_vma=False
    )
```

```python
import functools

import jax
import jax.numpy as jnp
from jax import lax
from jax.experimental import pallas as pl
from jax.experimental.pallas import tpu as pltpu
from jax.sharding import PartitionSpec as P

AXIS = "rows"
MESH = pl.DeviceIdType.MESH
ITERS = 4
BS = 128
NB = 128
HALF = 64
LEVELS = 5
LINKS = LEVELS * HALF
EDGE0 = NB
LINK0 = 2 * NB
SUMS = 3
PARTS = 16
F32 = jnp.float32
BF16 = jnp.bfloat16


def level_mask(li):
    q = li // 2
    return 8 * (1 + q + q // 2) * (1 + 7 * (li % 2))


def level_index(li):
    return 4 - li // 2 - 3 * (li % 2)


def level_partner(me, li):
    mask = level_mask(li)
    return me + mask - 2 * mask * ((me // mask) % 2)


def split_rows(d):
    high = d.astype(BF16).astype(F32)
    return jnp.concatenate([high, d - high], axis=0).astype(BF16)


def kernel(
    b_hbm, shift_hbm, dict_hbm, dids_hbm, gain_hbm, cids_hbm, cw_hbm, lrow_hbm, lids_hbm, lw_hbm,
    x_ref, r_ref,
    g_ref, stage, shift_ref, dids, cids, rows, lids, gain, cw, lrow, lw,
    wv, bw, st, upad, vecs, acc_ref, f_ref, ol_ref, scal,
    send, recv, csend, crecv, ar_src, ar_one, ar_mid, ar_two,
    in_sem, dict_sem, lv_s, lv_r, cy_s, cy_r, a1_s, a1_r, a2_s, a2_r,
):
    me = lax.axis_index(AXIS)
    n = lax.axis_size(AXIS)
    core, xs, zs, ys = me % 2, (me // 2) % 4, (me // 8) % 8, me // 64
    nxt, prv = (me + 1) % n, (me + n - 1) % n

    def one_peer(j):
        return ys * 64 + ((zs + j // 2) % 8) * 8 + xs * 2 + (core + j % 2) % 2

    def two_peer(j):
        return ((ys + j // 4) % 4) * 64 + zs * 8 + ((xs + j % 4) % 4) * 2 + core

    small = [
        pltpu.make_async_copy(src, dst, in_sem.at[i])
        for i, (src, dst) in enumerate((
            (b_hbm, upad.at[pl.ds(8, NB)]), (lrow_hbm, rows), (lrow_hbm, lrow), (shift_hbm, shift_ref),
            (gain_hbm, gain), (cw_hbm, cw), (lw_hbm, lw), (dids_hbm, dids), (cids_hbm, cids), (lids_hbm, lids),
        ))
    ]
    for copy in small:
        copy.start()

    def dict_copy(c):
        part = pl.ds(c * 8, 8)
        return pltpu.make_async_copy(dict_hbm.at[part], stage.at[part], dict_sem.at[c])

    @pl.loop(0, 16)
    def _(c):
        dict_copy(c).start()

    barrier = pltpu.get_barrier_semaphore()

    @pl.loop(1, PARTS)
    def _(j):
        pl.semaphore_signal(barrier, inc=1, device_id={AXIS: one_peer(j)}, device_id_type=MESH)
        pl.semaphore_signal(barrier, inc=1, device_id={AXIS: two_peer(j)}, device_id_type=MESH)

    pl.semaphore_signal(barrier, inc=1, device_id={AXIS: nxt}, device_id_type=MESH)
    pl.semaphore_signal(barrier, inc=1, device_id={AXIS: prv}, device_id_type=MESH)

    for copy in small:
        copy.wait()

    eye = lax.broadcasted_iota(jnp.int32, (NB, BS), 0) == lax.broadcasted_iota(jnp.int32, (NB, BS), 1)
    row_of = lax.broadcasted_iota(jnp.int32, (NB, BS), 0)

    def spread_rows(row):
        return jnp.broadcast_to(jnp.sum(jnp.where(eye, row, 0.0), axis=1, keepdims=True), (NB, BS))

    wv[0:NB, :] = spread_rows(gain[...])
    wv[EDGE0 : EDGE0 + NB, :] = spread_rows(cw[0:1, :])
    for blk in range(3):
        m0, m1 = level_index(2 * blk), level_index(min(2 * blk + 1, LEVELS - 1))
        lanes = slice(blk * BS, (blk + 1) * BS)
        wv[LINK0 + blk * NB : LINK0 + (blk + 1) * NB, :] = spread_rows(jnp.concatenate([lw[m0], lw[m1]], axis=1))
        second = lrow[m1] if blk < 2 else jnp.full((1, HALF), -1, jnp.int32)
        hit = row_of == jnp.concatenate([lrow[m0], second], axis=1)
        st[:, lanes] = jnp.where(hit, 1.0, 0.0).astype(BF16)
    bw[0:1, :] = wv[EDGE0 : EDGE0 + 1, :]
    bw[1:8, :] = jnp.broadcast_to(cw[1:2, BS - 1 :], (7, BS))
    upad[0:8, :] = jnp.zeros((8, BS), F32)
    ol_ref[LINKS:, :] = jnp.zeros((64, 2 * BS), F32)
    pl.semaphore_wait(barrier, 2 * (PARTS - 1) + 2)

    sub16 = lax.broadcasted_iota(jnp.int32, (16, BS), 0) % 8

    def products(d, picks):
        lhs = split_rows(d)
        out = jnp.zeros((16, 2 * BS), F32)
        for j, pick in enumerate(picks):
            picked = jnp.where(sub16 == j, lhs, jnp.zeros_like(lhs))
            out = out + jnp.dot(picked, g_ref[pick], preferred_element_type=F32)
        return (out[:8, :BS] + out[8:, BS:]) + (out[:8, BS:] + out[8:, :BS])

    def level_copy(k, li):
        return pltpu.make_async_remote_copy(
            src_ref=send.at[k, li], dst_ref=recv.at[k, li], send_sem=lv_s.at[k, li], recv_sem=lv_r.at[k, li],
            device_id={AXIS: level_partner(me, li)}, device_id_type=MESH)

    def cycle_copy(k, side):
        return pltpu.make_async_remote_copy(
            src_ref=csend.at[k, side], dst_ref=crecv.at[k, side], send_sem=cy_s.at[k, side],
            recv_sem=cy_r.at[k, side], device_id={AXIS: nxt if side == 0 else prv}, device_id_type=MESH)

    def one_copy(k, j):
        return pltpu.make_async_remote_copy(
            src_ref=ar_src.at[k], dst_ref=ar_one.at[k, j], send_sem=a1_s.at[k, j], recv_sem=a1_r.at[k, j],
            device_id={AXIS: one_peer(j)}, device_id_type=MESH)

    def two_copy(k, j):
        return pltpu.make_async_remote_copy(
            src_ref=ar_mid.at[k], dst_ref=ar_two.at[k, j], send_sem=a2_s.at[k, j], recv_sem=a2_r.at[k, j],
            device_id={AXIS: two_peer(j)}, device_id_type=MESH)

    def reduce_begin(k):
        @pl.loop(1, PARTS)
        def _(j):
            one_copy(k, j).start()

    def reduce_middle(k):
        @pl.loop(1, PARTS)
        def _(j):
            one_copy(k, j).wait()

        ar_one[k, 0] = ar_src[k]
        ar_mid[k] = jnp.sum(ar_one[k], axis=0)

        @pl.loop(1, PARTS)
        def _(j):
            two_copy(k, j).start()

    def reduce_end(k):
        @pl.loop(1, PARTS)
        def _(j):
            two_copy(k, j).wait()

        ar_two[k, 0] = ar_mid[k]
        return jnp.sum(ar_two[k], axis=0)

    def put_sums(k, pairs):
        count = -(-len(pairs) // 8) * 8
        parts = [jnp.sum(a * b, axis=0, keepdims=True) for a, b in pairs]
        parts += [jnp.zeros((1, BS), F32)] * (count - len(pairs))
        sums = jnp.sum(jnp.concatenate(parts, axis=0), axis=1, keepdims=True)
        shape = (count, BS)
        own = lax.broadcasted_iota(jnp.int32, shape, 0) == lax.broadcasted_iota(jnp.int32, shape, 1)
        ar_src[k] = jnp.sum(jnp.where(own, jnp.broadcast_to(sums, shape), 0.0), axis=0, keepdims=True)

    def lane(total, i):
        return jnp.broadcast_to(total[:, i : i + 1], (8, BS))

    def wide(value):
        return jnp.tile(value, (NB // 8, 1))

    def convert():
        @pl.loop(0, 16)
        def _(c):
            dict_copy(c).wait()

            @pl.loop(0, 2)
            def _(i):
                for j in range(4):
                    at = c * 8 + i * 4 + j
                    block = stage[at]
                    high = block.astype(BF16)
                    g_ref[at, :, 0:BS] = high
                    g_ref[at, :, BS:] = (block - high.astype(F32)).astype(BF16)

    def operate(k):
        @pl.loop(0, LEVELS)
        def _(i):
            li = LEVELS - 1 - i
            m = level_index(li)

            @pl.loop(0, HALF // 16)
            def _(h):
                for j in range(16):
                    row = rows[m, 0, h * 16 + j]
                    send[k, li, pl.ds(h * 16 + j, 1), :] = upad[pl.ds(row + 8, 1), :]

            level_copy(k, li).start()

        csend[k, 0] = upad[7 + NB : 8 + NB, :]
        csend[k, 1] = upad[8:9, :]
        cycle_copy(k, 0).start()
        cycle_copy(k, 1).start()

        @pl.when(k == 0)
        def _():
            convert()

        def local(t, carry):
            for part in range(4):
                g = pl.multiple_of(t * 32 + part * 8, 8)
                here = upad[pl.ds(g + 8, 8), :]
                before = upad[pl.ds(g + 7, 8), :]
                own = products(here * wv[pl.ds(g, 8), :], [dids[g + j] for j in range(8)])
                acc_ref[pl.ds(g, 8), :] = shift_ref[pl.ds(g, 8), :] * here + own
                edge = (here - before) * wv[pl.ds(EDGE0 + g, 8), :]
                f_ref[pl.ds(g, 8), :] = products(edge, [cids[0, g + j] for j in range(8)])
            return carry

        lax.fori_loop(0, 4, local, 0)

        def level(li, carry):
            level_copy(k, li).wait_recv()
            m = level_index(li)
            for h in range(8):
                c = pl.multiple_of(li * HALF + h * 8, 8)
                diff = send[k, li, h * 8 : h * 8 + 8, :] - recv[k, li, h * 8 : h * 8 + 8, :]
                out = products(diff * wv[pl.ds(LINK0 + c, 8), :], [lids[m, 0, h * 8 + j] for j in range(8)])
                high = out.astype(BF16).astype(F32)
                ol_ref[pl.ds(c, 8), 0:BS] = high
                ol_ref[pl.ds(c, 8), BS:] = out - high
            return carry

        lax.fori_loop(0, LEVELS, level, 0)
        cycle_copy(k, 0).wait()
        cycle_copy(k, 1).wait()
        sub8 = lax.broadcasted_iota(jnp.int32, (8, BS), 0)
        edge = jnp.where(sub8 == 0, upad[8:9, :] - crecv[k, 0], crecv[k, 1] - upad[7 + NB : 8 + NB, :])
        bound = products(edge * bw[...], [cids[0, 0], cids[1, NB - 1]])
        f_ref[0:1, :] = bound[0:1, :]
        f_ref[NB : NB + 1, :] = bound[1:2, :]
        spread = jnp.dot(st[...], ol_ref[...].astype(BF16), preferred_element_type=F32)
        acc_ref[...] = acc_ref[...] + (f_ref[0:NB, :] - f_ref[1 : NB + 1, :]) + (spread[:, :BS] + spread[:, BS:])

        @pl.loop(0, LEVELS)
        def _(li):
            level_copy(k, li).wait_send()

    vecs[0] = upad[8 : 8 + NB, :]

    def iteration(k, carry):
        operate(k)
        vecs[k + 1] = acc_ref[...]

        @pl.when(k < 2)
        def _():
            vec = upad[8 : 8 + NB, :]
            image = acc_ref[...]
            put_sums(k, [(vec, vec), (vec, image)])
            reduce_begin(k)
            upad[8 : 8 + NB, :] = image

        @pl.when((k == 1) | (k == 2))
        def _():
            reduce_middle(k - 1)

        @pl.when(k == 2)
        def _():
            total = reduce_end(0)
            scal[0] = lane(total, 0)
            scal[1] = lane(total, 1)
            upad[8 : 8 + NB, :] = vecs[2] - wide(scal[0] / scal[1]) * vecs[3]

        return carry

    lax.fori_loop(0, ITERS, iteration, 0)
    total = reduce_end(1)
    m0, m1, m2, m3 = scal[0], scal[1], lane(total, 0), lane(total, 1)
    alpha0 = m0 / m1
    norm1 = m0 - 2.0 * alpha0 * m1 + alpha0 * alpha0 * m2
    product1 = m1 - 2.0 * alpha0 * m2 + alpha0 * alpha0 * m3
    beta1 = norm1 / m0
    alpha1 = norm1 / (product1 - beta1 * norm1 / alpha0)
    al0, al1, be1 = wide(alpha0), wide(alpha1), wide(beta1)
    r1 = vecs[0] - al0 * vecs[1]
    w1 = vecs[1] - al0 * vecs[2]
    n1 = upad[8 : 8 + NB, :]
    p1 = r1 + be1 * vecs[0]
    s1 = w1 + be1 * vecs[1]
    z1 = n1 + be1 * vecs[2]
    x_ref[...] = al0 * vecs[0] + al1 * p1
    r2 = r1 - al1 * s1
    w2 = w1 - al1 * z1
    n2 = n1 - al1 * (vecs[4] + be1 * vecs[3])
    put_sums(2, [(r2, r2), (r2, w2), (w2, w2), (r2, s1), (w2, s1), (s1, s1), (r2, n2), (r2, z1), (w2, n2), (w2, z1),
                 (s1, n2), (s1, z1)])
    vecs[0] = p1
    vecs[1] = s1
    vecs[2] = z1
    r_ref[...] = r2
    vecs[3] = w2
    vecs[4] = n2
    reduce_begin(2)
    reduce_middle(2)
    total = reduce_end(2)
    rr, rw, ww, rs, ws, ss, rn, rz, wn, wz, sn, sz = (lane(total, i) for i in range(12))
    beta2 = rr / norm1
    alpha2 = rr / (rw - beta2 * rr / alpha1)
    c, d = alpha2, alpha2 * beta2
    norm3 = rr + c * c * ww + d * d * ss - 2.0 * (c * rw + d * rs - c * d * ws)
    product3 = rw - c * (rn + ww) - d * (rz + ws) + c * c * wn + c * d * (wz + sn) + d * d * sz
    beta3 = norm3 / rr
    alpha3 = norm3 / (product3 - beta3 * norm3 / alpha2)
    al2, be2, al3, be3 = wide(alpha2), wide(beta2), wide(alpha3), wide(beta3)
    p2 = r_ref[...] + be2 * vecs[0]
    s2 = vecs[3] + be2 * vecs[1]
    r3 = r_ref[...] - al2 * s2
    w3 = vecs[3] - al2 * (vecs[4] + be2 * vecs[2])
    x_ref[...] = x_ref[...] + al2 * p2 + al3 * (r3 + be3 * p2)
    r_ref[...] = r3 - al3 * (w3 + be3 * s2)


def per_device(
    right_side,
    diag_shift,
    dictionary,
    diag_ids,
    diag_gain,
    cycle_ids,
    cycle_weights,
    link_rows,
    link_ids,
    link_weights,
):

    vec = (NB, BS)
    across = (1, 0, 2)
    vmem = pl.BlockSpec(memory_space=pltpu.VMEM)
    args = (
        right_side.reshape(vec), diag_shift.reshape(vec), dictionary, diag_ids, diag_gain.reshape(1, NB),
        cycle_ids.T, cycle_weights.T, jnp.transpose(link_rows, across), jnp.transpose(link_ids, across),
        jnp.transpose(link_weights, across),
    )
    solved, residual = pl.pallas_call(
        kernel,
        out_shape=(jax.ShapeDtypeStruct(vec, F32), jax.ShapeDtypeStruct(vec, F32)),
        in_specs=[pl.BlockSpec(memory_space=pl.ANY)] * len(args),
        out_specs=(vmem, vmem),
        scratch_shapes=[
            pltpu.VMEM((BS, BS, 2 * BS), BF16),
            pltpu.VMEM((BS, BS, BS), F32),
            pltpu.VMEM(vec, F32),
            pltpu.SMEM((NB,), jnp.int32),
            pltpu.SMEM((2, NB), jnp.int32),
            pltpu.SMEM((LEVELS, 1, HALF), jnp.int32),
            pltpu.SMEM((LEVELS, 1, HALF), jnp.int32),
            pltpu.VMEM((1, NB), F32),
            pltpu.VMEM((2, NB), F32),
            pltpu.VMEM((LEVELS, 1, HALF), jnp.int32),
            pltpu.VMEM((LEVELS, 1, HALF), F32),
            pltpu.VMEM((LINK0 + 3 * NB, BS), F32),
            pltpu.VMEM((8, BS), F32),
            pltpu.VMEM((NB, 3 * BS), BF16),
            pltpu.VMEM((NB + 8, BS), F32),
            pltpu.VMEM((ITERS + 1, NB, BS), F32),
            pltpu.VMEM(vec, F32),
            pltpu.VMEM((NB + 8, BS), F32),
            pltpu.VMEM((3 * BS, 2 * BS), F32),
            pltpu.VMEM((2, 8, BS), F32),
            pltpu.VMEM((ITERS, LEVELS, HALF, BS), F32),
            pltpu.VMEM((ITERS, LEVELS, HALF, BS), F32),
            pltpu.VMEM((ITERS, 2, 1, BS), F32),
            pltpu.VMEM((ITERS, 2, 1, BS), F32),
            pltpu.VMEM((SUMS, 1, BS), F32),
            pltpu.VMEM((SUMS, PARTS, 1, BS), F32),
            pltpu.VMEM((SUMS, 1, BS), F32),
            pltpu.VMEM((SUMS, PARTS, 1, BS), F32),
            pltpu.SemaphoreType.DMA((len(args),)),
            pltpu.SemaphoreType.DMA((16,)),
            pltpu.SemaphoreType.DMA((ITERS, LEVELS)),
            pltpu.SemaphoreType.DMA((ITERS, LEVELS)),
            pltpu.SemaphoreType.DMA((ITERS, 2)),
            pltpu.SemaphoreType.DMA((ITERS, 2)),
            pltpu.SemaphoreType.DMA((SUMS, PARTS)),
            pltpu.SemaphoreType.DMA((SUMS, PARTS)),
            pltpu.SemaphoreType.DMA((SUMS, PARTS)),
            pltpu.SemaphoreType.DMA((SUMS, PARTS)),
        ],
        compiler_params=pltpu.CompilerParams(
            collective_id=0, has_side_effects=True, vmem_limit_bytes=58 * 1024 * 1024
        ),
        name="cg",
    )(*args)
    return solved.reshape(-1), residual.reshape(-1)


def solution(mesh):
    placed = (
        P(AXIS),
        P(AXIS),
        P(),
        P(AXIS),
        P(AXIS),
        P(AXIS, None),
        P(AXIS, None),
        P(AXIS, None, None),
        P(AXIS, None, None),
        P(AXIS, None, None),
    )
    return jax.shard_map(
        per_device, mesh=mesh, in_specs=placed, out_specs=(P(AXIS), P(AXIS)), check_vma=False
    )
```

```python
import functools

import jax
import jax.numpy as jnp
from jax import lax
from jax.experimental import pallas as pl
from jax.experimental.pallas import tpu as pltpu
from jax.sharding import PartitionSpec as P

AXIS = "rows"
MESH = pl.DeviceIdType.MESH
ITERS = 4
BS = 128
NB = 128
HALF = 64
LEVELS = 5
LINKS = LEVELS * HALF
EDGE0 = NB
LINK0 = 2 * NB
SUMS = 3
PARTS = 16
F32 = jnp.float32
BF16 = jnp.bfloat16


def level_mask(li):
    q = li // 2
    return 8 * (1 + q + q // 2) * (1 + 7 * (li % 2))


def level_index(li):
    return 4 - li // 2 - 3 * (li % 2)


def level_partner(me, li):
    mask = level_mask(li)
    return me + mask - 2 * mask * ((me // mask) % 2)


def split_rows(d):
    high = d.astype(BF16).astype(F32)
    return jnp.concatenate([high, d - high], axis=0).astype(BF16)


def kernel(
    b_hbm, shift_hbm, dict_hbm, dids_hbm, gain_hbm, cids_hbm, cw_hbm, lrow_hbm, lids_hbm, lw_hbm,
    out_ref,
    g_ref, stage, shift_ref, dids, cids, rows, lids, gain, cw, lrow, lw,
    wv, bw, st, upad, vecs, acc_ref, f_ref, ol_ref, scal,
    send, recv, csend, crecv, ar_src, ar_one, ar_mid, ar_two,
    in_sem, dict_sem, lv_s, lv_r, cy_s, cy_r, a1_s, a1_r, a2_s, a2_r,
):
    me = lax.axis_index(AXIS)
    n = lax.axis_size(AXIS)
    core, xs, zs, ys = me % 2, (me // 2) % 4, (me // 8) % 8, me // 64
    nxt, prv = (me + 1) % n, (me + n - 1) % n

    def one_peer(j):
        return ys * 64 + ((zs + j // 2) % 8) * 8 + xs * 2 + (core + j % 2) % 2

    def two_peer(j):
        return ((ys + j // 4) % 4) * 64 + zs * 8 + ((xs + j % 4) % 4) * 2 + core

    small = [
        pltpu.make_async_copy(src, dst, in_sem.at[i])
        for i, (src, dst) in enumerate((
            (b_hbm, upad.at[pl.ds(8, NB)]), (lrow_hbm, rows), (lrow_hbm, lrow), (shift_hbm, shift_ref),
            (gain_hbm, gain), (cw_hbm, cw), (lw_hbm, lw), (dids_hbm, dids), (cids_hbm, cids), (lids_hbm, lids),
        ))
    ]
    for copy in small:
        copy.start()

    def dict_copy(c):
        part = pl.ds(c * 8, 8)
        return pltpu.make_async_copy(dict_hbm.at[part], stage.at[part], dict_sem.at[c])

    @pl.loop(0, 16)
    def _(c):
        dict_copy(c).start()

    barrier = pltpu.get_barrier_semaphore()

    @pl.loop(1, PARTS)
    def _(j):
        pl.semaphore_signal(barrier, inc=1, device_id={AXIS: one_peer(j)}, device_id_type=MESH)
        pl.semaphore_signal(barrier, inc=1, device_id={AXIS: two_peer(j)}, device_id_type=MESH)

    pl.semaphore_signal(barrier, inc=1, device_id={AXIS: nxt}, device_id_type=MESH)
    pl.semaphore_signal(barrier, inc=1, device_id={AXIS: prv}, device_id_type=MESH)

    for copy in small:
        copy.wait()

    eye = lax.broadcasted_iota(jnp.int32, (NB, BS), 0) == lax.broadcasted_iota(jnp.int32, (NB, BS), 1)
    row_of = lax.broadcasted_iota(jnp.int32, (NB, BS), 0)

    def spread_rows(row):
        return jnp.broadcast_to(jnp.sum(jnp.where(eye, row, 0.0), axis=1, keepdims=True), (NB, BS))

    wv[0:NB, :] = spread_rows(gain[...])
    wv[EDGE0 : EDGE0 + NB, :] = spread_rows(cw[0:1, :])
    for blk in range(3):
        m0, m1 = level_index(2 * blk), level_index(min(2 * blk + 1, LEVELS - 1))
        lanes = slice(blk * BS, (blk + 1) * BS)
        wv[LINK0 + blk * NB : LINK0 + (blk + 1) * NB, :] = spread_rows(jnp.concatenate([lw[m0], lw[m1]], axis=1))
        second = lrow[m1] if blk < 2 else jnp.full((1, HALF), -1, jnp.int32)
        hit = row_of == jnp.concatenate([lrow[m0], second], axis=1)
        st[:, lanes] = jnp.where(hit, 1.0, 0.0).astype(BF16)
    bw[0:1, :] = wv[EDGE0 : EDGE0 + 1, :]
    bw[1:8, :] = jnp.broadcast_to(cw[1:2, BS - 1 :], (7, BS))
    upad[0:8, :] = jnp.zeros((8, BS), F32)
    ol_ref[LINKS:, :] = jnp.zeros((64, 2 * BS), F32)
    pl.semaphore_wait(barrier, 2 * (PARTS - 1) + 2)

    sub16 = lax.broadcasted_iota(jnp.int32, (16, BS), 0) % 8

    def products(d, picks):
        lhs = split_rows(d)
        out = jnp.zeros((16, 2 * BS), F32)
        for j, pick in enumerate(picks):
            picked = jnp.where(sub16 == j, lhs, jnp.zeros_like(lhs))
            out = out + jnp.dot(picked, g_ref[pick], preferred_element_type=F32)
        return (out[:8, :BS] + out[8:, BS:]) + (out[:8, BS:] + out[8:, :BS])

    def level_copy(k, li):
        return pltpu.make_async_remote_copy(
            src_ref=send.at[k, li], dst_ref=recv.at[k, li], send_sem=lv_s.at[k, li], recv_sem=lv_r.at[k, li],
            device_id={AXIS: level_partner(me, li)}, device_id_type=MESH)

    def cycle_copy(k, side):
        return pltpu.make_async_remote_copy(
            src_ref=csend.at[k, side], dst_ref=crecv.at[k, side], send_sem=cy_s.at[k, side],
            recv_sem=cy_r.at[k, side], device_id={AXIS: nxt if side == 0 else prv}, device_id_type=MESH)

    def one_copy(k, j):
        return pltpu.make_async_remote_copy(
            src_ref=ar_src.at[k], dst_ref=ar_one.at[k, j], send_sem=a1_s.at[k, j], recv_sem=a1_r.at[k, j],
            device_id={AXIS: one_peer(j)}, device_id_type=MESH)

    def two_copy(k, j):
        return pltpu.make_async_remote_copy(
            src_ref=ar_mid.at[k], dst_ref=ar_two.at[k, j], send_sem=a2_s.at[k, j], recv_sem=a2_r.at[k, j],
            device_id={AXIS: two_peer(j)}, device_id_type=MESH)

    def reduce_begin(k):
        for j in sorted(range(1, PARTS), key=lambda j: abs(j // 2 - 4)):
            one_copy(k, j).start()

    def reduce_middle(k):
        @pl.loop(1, PARTS)
        def _(j):
            one_copy(k, j).wait()

        ar_one[k, 0] = ar_src[k]
        ar_mid[k] = jnp.sum(ar_one[k], axis=0)

        for j in sorted(range(1, PARTS), key=lambda j: abs(j // 4 - 2) + abs(j % 4 - 2)):
            two_copy(k, j).start()

    def reduce_end(k):
        @pl.loop(1, PARTS)
        def _(j):
            two_copy(k, j).wait()

        ar_two[k, 0] = ar_mid[k]
        return jnp.sum(ar_two[k], axis=0)

    def put_sums(k, pairs):
        count = -(-len(pairs) // 8) * 8
        parts = [jnp.sum(a * b, axis=0, keepdims=True) for a, b in pairs]
        parts += [jnp.zeros((1, BS), F32)] * (count - len(pairs))
        sums = jnp.sum(jnp.concatenate(parts, axis=0), axis=1, keepdims=True)
        shape = (count, BS)
        own = lax.broadcasted_iota(jnp.int32, shape, 0) == lax.broadcasted_iota(jnp.int32, shape, 1)
        ar_src[k] = jnp.sum(jnp.where(own, jnp.broadcast_to(sums, shape), 0.0), axis=0, keepdims=True)

    def lane(total, i):
        return jnp.broadcast_to(total[:, i : i + 1], (8, BS))

    def wide(value):
        return jnp.tile(value, (NB // 8, 1))

    def convert():
        @pl.loop(0, 16)
        def _(c):
            dict_copy(c).wait()

            @pl.loop(0, 2)
            def _(i):
                for j in range(4):
                    at = c * 8 + i * 4 + j
                    block = stage[at]
                    high = block.astype(BF16)
                    g_ref[at, :, 0:BS] = high
                    g_ref[at, :, BS:] = (block - high.astype(F32)).astype(BF16)

    def operate(k):
        @pl.loop(0, LEVELS)
        def _(i):
            li = LEVELS - 1 - i
            m = level_index(li)

            @pl.loop(0, HALF // 32)
            def _(h):
                found = [upad[pl.ds(rows[m, 0, h * 32 + j] + 8, 1), :] for j in range(32)]
                for j in range(32):
                    send[k, li, pl.ds(h * 32 + j, 1), :] = found[j]

            level_copy(k, li).start()

        csend[k, 0] = upad[7 + NB : 8 + NB, :]
        csend[k, 1] = upad[8:9, :]
        cycle_copy(k, 0).start()
        cycle_copy(k, 1).start()

        @pl.when(k == 0)
        def _():
            convert()

        def local(t, carry):
            for part in range(8):
                g = pl.multiple_of(t * 64 + part * 8, 8)
                here = upad[pl.ds(g + 8, 8), :]
                before = upad[pl.ds(g + 7, 8), :]
                own = products(here * wv[pl.ds(g, 8), :], [dids[g + j] for j in range(8)])
                acc_ref[pl.ds(g, 8), :] = shift_ref[pl.ds(g, 8), :] * here + own
                edge = (here - before) * wv[pl.ds(EDGE0 + g, 8), :]
                f_ref[pl.ds(g, 8), :] = products(edge, [cids[0, g + j] for j in range(8)])
            return carry

        lax.fori_loop(0, 2, local, 0)

        def level(li):
            m = level_index(li)
            for h in range(8):
                c = pl.multiple_of(li * HALF + h * 8, 8)
                diff = send[k, li, h * 8 : h * 8 + 8, :] - recv[k, li, h * 8 : h * 8 + 8, :]
                out = products(diff * wv[pl.ds(LINK0 + c, 8), :], [lids[m, 0, h * 8 + j] for j in range(8)])
                high = out.astype(BF16).astype(F32)
                ol_ref[pl.ds(c, 8), 0:BS] = high
                ol_ref[pl.ds(c, 8), BS:] = out - high

        def two_levels(i, carry):
            level_copy(k, 2 * i).wait_recv()
            level_copy(k, 2 * i + 1).wait_recv()
            level(2 * i)
            level(2 * i + 1)
            return carry

        lax.fori_loop(0, LEVELS // 2, two_levels, 0)
        level_copy(k, LEVELS - 1).wait_recv()
        level(LEVELS - 1)
        cycle_copy(k, 0).wait()
        cycle_copy(k, 1).wait()
        sub8 = lax.broadcasted_iota(jnp.int32, (8, BS), 0)
        edge = jnp.where(sub8 == 0, upad[8:9, :] - crecv[k, 0], crecv[k, 1] - upad[7 + NB : 8 + NB, :])
        bound = products(edge * bw[...], [cids[0, 0], cids[1, NB - 1]])
        f_ref[0:1, :] = bound[0:1, :]
        f_ref[NB : NB + 1, :] = bound[1:2, :]
        spread = jnp.dot(st[...], ol_ref[...].astype(BF16), preferred_element_type=F32)
        acc_ref[...] = acc_ref[...] + (f_ref[0:NB, :] - f_ref[1 : NB + 1, :]) + (spread[:, :BS] + spread[:, BS:])

        @pl.loop(0, LEVELS)
        def _(li):
            level_copy(k, li).wait_send()

    vecs[0] = upad[8 : 8 + NB, :]

    def iteration(k, carry):
        operate(k)
        vecs[k + 1] = acc_ref[...]

        @pl.when(k < 2)
        def _():
            vec = upad[8 : 8 + NB, :]
            image = acc_ref[...]
            put_sums(k, [(vec, vec), (vec, image)])
            reduce_begin(k)
            upad[8 : 8 + NB, :] = image

        @pl.when((k == 1) | (k == 2))
        def _():
            reduce_middle(k - 1)

        @pl.when(k == 2)
        def _():
            total = reduce_end(0)
            scal[0] = lane(total, 0)
            scal[1] = lane(total, 1)
            upad[8 : 8 + NB, :] = vecs[2] - wide(scal[0] / scal[1]) * vecs[3]

        return carry

    lax.fori_loop(0, ITERS, iteration, 0)
    total = reduce_end(1)
    m0, m1, m2, m3 = scal[0], scal[1], lane(total, 0), lane(total, 1)
    alpha0 = m0 / m1
    norm1 = m0 - 2.0 * alpha0 * m1 + alpha0 * alpha0 * m2
    product1 = m1 - 2.0 * alpha0 * m2 + alpha0 * alpha0 * m3
    beta1 = norm1 / m0
    alpha1 = norm1 / (product1 - beta1 * norm1 / alpha0)
    al0, al1, be1 = wide(alpha0), wide(alpha1), wide(beta1)
    r1 = vecs[0] - al0 * vecs[1]
    w1 = vecs[1] - al0 * vecs[2]
    n1 = upad[8 : 8 + NB, :]
    p1 = r1 + be1 * vecs[0]
    s1 = w1 + be1 * vecs[1]
    z1 = n1 + be1 * vecs[2]
    out_ref[0] = al0 * vecs[0] + al1 * p1
    r2 = r1 - al1 * s1
    w2 = w1 - al1 * z1
    n2 = n1 - al1 * (vecs[4] + be1 * vecs[3])
    put_sums(2, [(r2, r2), (r2, w2), (w2, w2), (r2, s1), (w2, s1), (s1, s1), (r2, n2), (r2, z1), (w2, n2), (w2, z1),
                 (s1, n2), (s1, z1)])
    vecs[0] = p1
    vecs[1] = s1
    vecs[2] = z1
    out_ref[1] = r2
    vecs[3] = w2
    vecs[4] = n2
    reduce_begin(2)
    reduce_middle(2)
    total = reduce_end(2)
    rr, rw, ww, rs, ws, ss, rn, rz, wn, wz, sn, sz = (lane(total, i) for i in range(12))
    beta2 = rr / norm1
    alpha2 = rr / (rw - beta2 * rr / alpha1)
    c, d = alpha2, alpha2 * beta2
    norm3 = rr + c * c * ww + d * d * ss - 2.0 * (c * rw + d * rs - c * d * ws)
    product3 = rw - c * (rn + ww) - d * (rz + ws) + c * c * wn + c * d * (wz + sn) + d * d * sz
    beta3 = norm3 / rr
    alpha3 = norm3 / (product3 - beta3 * norm3 / alpha2)
    al2, be2, al3, be3 = wide(alpha2), wide(beta2), wide(alpha3), wide(beta3)
    p2 = out_ref[1] + be2 * vecs[0]
    s2 = vecs[3] + be2 * vecs[1]
    r3 = out_ref[1] - al2 * s2
    w3 = vecs[3] - al2 * (vecs[4] + be2 * vecs[2])
    out_ref[0] = out_ref[0] + al2 * p2 + al3 * (r3 + be3 * p2)
    out_ref[1] = r3 - al3 * (w3 + be3 * s2)


def per_device(
    right_side,
    diag_shift,
    dictionary,
    diag_ids,
    diag_gain,
    cycle_ids,
    cycle_weights,
    link_rows,
    link_ids,
    link_weights,
):

    vec = (NB, BS)
    across = (1, 0, 2)
    vmem = pl.BlockSpec(memory_space=pltpu.VMEM)
    args = (
        right_side.reshape(vec), diag_shift.reshape(vec), dictionary, diag_ids, diag_gain.reshape(1, NB),
        cycle_ids.T, cycle_weights.T, jnp.transpose(link_rows, across), jnp.transpose(link_ids, across),
        jnp.transpose(link_weights, across),
    )
    out = pl.pallas_call(
        kernel,
        out_shape=jax.ShapeDtypeStruct((2, *vec), F32),
        in_specs=[pl.BlockSpec(memory_space=pl.ANY)] * len(args),
        out_specs=vmem,
        scratch_shapes=[
            pltpu.VMEM((BS, BS, 2 * BS), BF16),
            pltpu.VMEM((BS, BS, BS), F32),
            pltpu.VMEM(vec, F32),
            pltpu.SMEM((NB,), jnp.int32),
            pltpu.SMEM((2, NB), jnp.int32),
            pltpu.SMEM((LEVELS, 1, HALF), jnp.int32),
            pltpu.SMEM((LEVELS, 1, HALF), jnp.int32),
            pltpu.VMEM((1, NB), F32),
            pltpu.VMEM((2, NB), F32),
            pltpu.VMEM((LEVELS, 1, HALF), jnp.int32),
            pltpu.VMEM((LEVELS, 1, HALF), F32),
            pltpu.VMEM((LINK0 + 3 * NB, BS), F32),
            pltpu.VMEM((8, BS), F32),
            pltpu.VMEM((NB, 3 * BS), BF16),
            pltpu.VMEM((NB + 8, BS), F32),
            pltpu.VMEM((ITERS + 1, NB, BS), F32),
            pltpu.VMEM(vec, F32),
            pltpu.VMEM((NB + 8, BS), F32),
            pltpu.VMEM((3 * BS, 2 * BS), F32),
            pltpu.VMEM((2, 8, BS), F32),
            pltpu.VMEM((ITERS, LEVELS, HALF, BS), F32),
            pltpu.VMEM((ITERS, LEVELS, HALF, BS), F32),
            pltpu.VMEM((ITERS, 2, 1, BS), F32),
            pltpu.VMEM((ITERS, 2, 1, BS), F32),
            pltpu.VMEM((SUMS, 1, BS), F32),
            pltpu.VMEM((SUMS, PARTS, 1, BS), F32),
            pltpu.VMEM((SUMS, 1, BS), F32),
            pltpu.VMEM((SUMS, PARTS, 1, BS), F32),
            pltpu.SemaphoreType.DMA((len(args),)),
            pltpu.SemaphoreType.DMA((16,)),
            pltpu.SemaphoreType.DMA((ITERS, LEVELS)),
            pltpu.SemaphoreType.DMA((ITERS, LEVELS)),
            pltpu.SemaphoreType.DMA((ITERS, 2)),
            pltpu.SemaphoreType.DMA((ITERS, 2)),
            pltpu.SemaphoreType.DMA((SUMS, PARTS)),
            pltpu.SemaphoreType.DMA((SUMS, PARTS)),
            pltpu.SemaphoreType.DMA((SUMS, PARTS)),
            pltpu.SemaphoreType.DMA((SUMS, PARTS)),
        ],
        compiler_params=pltpu.CompilerParams(
            collective_id=0, has_side_effects=True, vmem_limit_bytes=58 * 1024 * 1024
        ),
        name="cg",
    )(*args)
    return out[0].reshape(-1), out[1].reshape(-1)


def solution(mesh):
    placed = (
        P(AXIS),
        P(AXIS),
        P(),
        P(AXIS),
        P(AXIS),
        P(AXIS, None),
        P(AXIS, None),
        P(AXIS, None, None),
        P(AXIS, None, None),
        P(AXIS, None, None),
    )
    return jax.shard_map(
        per_device, mesh=mesh, in_specs=placed, out_specs=(P(AXIS), P(AXIS)), check_vma=False
    )
```

```python
import functools

import jax
import jax.numpy as jnp
from jax import lax
from jax.experimental import pallas as pl
from jax.experimental.pallas import tpu as pltpu
from jax.sharding import PartitionSpec as P

AXIS = "rows"
MESH = pl.DeviceIdType.MESH
ITERS = 4
BS = 128
NB = 128
HALF = 64
LEVELS = 5
LINKS = LEVELS * HALF
EDGE0 = NB
LINK0 = 2 * NB
SUMS = 3
PARTS = 16
F32 = jnp.float32
BF16 = jnp.bfloat16


def level_mask(li):
    q = li // 2
    return 8 * (1 + q + q // 2) * (1 + 7 * (li % 2))


def level_index(li):
    return 4 - li // 2 - 3 * (li % 2)


def level_partner(me, li):
    mask = level_mask(li)
    return me + mask - 2 * mask * ((me // mask) % 2)


def split_rows(d):
    high = d.astype(BF16).astype(F32)
    return jnp.concatenate([high, d - high], axis=0).astype(BF16)


def kernel(
    b_hbm, shift_hbm, dict_hbm, dids_hbm, gain_hbm, cids_hbm, cw_hbm, lrow_hbm, lids_hbm, lw_hbm,
    out_ref,
    g_ref, stage, shift_ref, dids, cids, rows, lids, gain, cw, lrow, lw,
    wv, bw, st, upad, vecs, acc_ref, f_ref, ol_ref, scal, kept, part_sums,
    send, recv, csend, crecv, ar_src, ar_one, ar_mid, ar_two,
    in_sem, dict_sem, lv_s, lv_r, cy_s, cy_r, a1_s, a1_r, a2_s, a2_r,
):
    me = lax.axis_index(AXIS)
    n = lax.axis_size(AXIS)
    core, xs, zs, ys = me % 2, (me // 2) % 4, (me // 8) % 8, me // 64
    nxt, prv = (me + 1) % n, (me + n - 1) % n

    def one_peer(j):
        return ys * 64 + ((zs + j // 2) % 8) * 8 + xs * 2 + (core + j % 2) % 2

    def two_peer(j):
        return ((ys + j // 4) % 4) * 64 + zs * 8 + ((xs + j % 4) % 4) * 2 + core

    small = [
        pltpu.make_async_copy(src, dst, in_sem.at[i])
        for i, (src, dst) in enumerate((
            (b_hbm, upad.at[pl.ds(8, NB)]), (lrow_hbm, rows), (lrow_hbm, lrow), (shift_hbm, shift_ref),
            (gain_hbm, gain), (cw_hbm, cw), (lw_hbm, lw), (dids_hbm, dids), (cids_hbm, cids), (lids_hbm, lids),
        ))
    ]
    for copy in small:
        copy.start()

    def dict_copy(c):
        part = pl.ds(c * 8, 8)
        return pltpu.make_async_copy(dict_hbm.at[part], stage.at[part], dict_sem.at[c])

    @pl.loop(0, 16)
    def _(c):
        dict_copy(c).start()

    barrier = pltpu.get_barrier_semaphore()

    @pl.loop(1, PARTS)
    def _(j):
        pl.semaphore_signal(barrier, inc=1, device_id={AXIS: one_peer(j)}, device_id_type=MESH)
        pl.semaphore_signal(barrier, inc=1, device_id={AXIS: two_peer(j)}, device_id_type=MESH)

    pl.semaphore_signal(barrier, inc=1, device_id={AXIS: nxt}, device_id_type=MESH)
    pl.semaphore_signal(barrier, inc=1, device_id={AXIS: prv}, device_id_type=MESH)

    for copy in small:
        copy.wait()

    eye = lax.broadcasted_iota(jnp.int32, (NB, BS), 0) == lax.broadcasted_iota(jnp.int32, (NB, BS), 1)
    row_of = lax.broadcasted_iota(jnp.int32, (NB, BS), 0)

    def spread_rows(row):
        return jnp.broadcast_to(jnp.sum(jnp.where(eye, row, 0.0), axis=1, keepdims=True), (NB, BS))

    wv[0:NB, :] = spread_rows(gain[...])
    wv[EDGE0 : EDGE0 + NB, :] = spread_rows(cw[0:1, :])
    for blk in range(3):
        m0, m1 = level_index(2 * blk), level_index(min(2 * blk + 1, LEVELS - 1))
        lanes = slice(blk * BS, (blk + 1) * BS)
        wv[LINK0 + blk * NB : LINK0 + (blk + 1) * NB, :] = spread_rows(jnp.concatenate([lw[m0], lw[m1]], axis=1))
        second = lrow[m1] if blk < 2 else jnp.full((1, HALF), -1, jnp.int32)
        hit = row_of == jnp.concatenate([lrow[m0], second], axis=1)
        st[:, lanes] = jnp.where(hit, 1.0, 0.0).astype(BF16)
    bw[0:1, :] = wv[EDGE0 : EDGE0 + 1, :]
    bw[1:8, :] = jnp.broadcast_to(cw[1:2, BS - 1 :], (7, BS))
    upad[0:8, :] = jnp.zeros((8, BS), F32)
    ol_ref[LINKS:, :] = jnp.zeros((64, 2 * BS), F32)
    pl.semaphore_wait(barrier, 2 * (PARTS - 1) + 2)

    sub16 = lax.broadcasted_iota(jnp.int32, (16, BS), 0) % 8

    def products(d, picks):
        lhs = split_rows(d)
        out = jnp.zeros((16, 2 * BS), F32)
        for j, pick in enumerate(picks):
            picked = jnp.where(sub16 == j, lhs, jnp.zeros_like(lhs))
            out = out + jnp.dot(picked, g_ref[pick], preferred_element_type=F32)
        return (out[:8, :BS] + out[8:, BS:]) + (out[:8, BS:] + out[8:, :BS])

    def level_copy(k, li):
        return pltpu.make_async_remote_copy(
            src_ref=send.at[k, li], dst_ref=recv.at[k, li], send_sem=lv_s.at[k, li], recv_sem=lv_r.at[k, li],
            device_id={AXIS: level_partner(me, li)}, device_id_type=MESH)

    def cycle_copy(k, side):
        return pltpu.make_async_remote_copy(
            src_ref=csend.at[k, side], dst_ref=crecv.at[k, side], send_sem=cy_s.at[k, side],
            recv_sem=cy_r.at[k, side], device_id={AXIS: nxt if side == 0 else prv}, device_id_type=MESH)

    def one_copy(k, j):
        return pltpu.make_async_remote_copy(
            src_ref=ar_src.at[k], dst_ref=ar_one.at[k, j], send_sem=a1_s.at[k, j], recv_sem=a1_r.at[k, j],
            device_id={AXIS: one_peer(j)}, device_id_type=MESH)

    def two_copy(k, j):
        return pltpu.make_async_remote_copy(
            src_ref=ar_mid.at[k], dst_ref=ar_two.at[k, j], send_sem=a2_s.at[k, j], recv_sem=a2_r.at[k, j],
            device_id={AXIS: two_peer(j)}, device_id_type=MESH)

    def reduce_begin(k):
        for j in sorted(range(1, PARTS), key=lambda j: abs(j // 2 - 4)):
            one_copy(k, j).start()

    def reduce_middle(k):
        for j in range(1, PARTS):
            one_copy(k, j).wait_recv()
        ar_one[k, 0] = ar_src[k]
        ar_mid[k] = jnp.sum(ar_one[k], axis=0)

        for j in sorted(range(1, PARTS), key=lambda j: abs(j // 4 - 2) + abs(j % 4 - 2)):
            two_copy(k, j).start()
        for j in range(1, PARTS):
            one_copy(k, j).wait_send()

    def reduce_end(k):
        for j in range(1, PARTS):
            two_copy(k, j).wait()
        ar_two[k, 0] = ar_mid[k]
        return jnp.sum(ar_two[k], axis=0)

    def row_sums(a, b):
        return jnp.sum(a * b, axis=0, keepdims=True)

    def put_sums(k, parts):
        count = -(-len(parts) // 8) * 8
        parts = parts + [jnp.zeros((1, BS), F32)] * (count - len(parts))
        sums = jnp.sum(jnp.concatenate(parts, axis=0), axis=1, keepdims=True)
        shape = (count, BS)
        own = lax.broadcasted_iota(jnp.int32, shape, 0) == lax.broadcasted_iota(jnp.int32, shape, 1)
        ar_src[k] = jnp.sum(jnp.where(own, jnp.broadcast_to(sums, shape), 0.0), axis=0, keepdims=True)

    def lane(total, i):
        return jnp.broadcast_to(total[:, i : i + 1], (8, BS))

    def wide(value):
        return jnp.tile(value, (NB // 8, 1))

    def convert():
        @pl.loop(0, 16)
        def _(c):
            dict_copy(c).wait()

            @pl.loop(0, 2)
            def _(i):
                for j in range(4):
                    at = c * 8 + i * 4 + j
                    block = stage[at]
                    high = block.astype(BF16)
                    g_ref[at, :, 0:BS] = high
                    g_ref[at, :, BS:] = (block - high.astype(F32)).astype(BF16)

    def prepare():
        total = reduce_end(1)
        m0, m1, m2, m3 = scal[0], scal[1], lane(total, 0), lane(total, 1)
        alpha0 = m0 / m1
        norm1 = m0 - 2.0 * alpha0 * m1 + alpha0 * alpha0 * m2
        product1 = m1 - 2.0 * alpha0 * m2 + alpha0 * alpha0 * m3
        beta1 = norm1 / m0
        alpha1 = norm1 / (product1 - beta1 * norm1 / alpha0)
        scal[2] = norm1
        scal[3] = alpha1
        al0, al1, be1 = wide(alpha0), wide(alpha1), wide(beta1)
        r1 = vecs[0] - al0 * vecs[1]
        w1 = vecs[1] - al0 * vecs[2]
        n1 = upad[8 : 8 + NB, :]
        p1 = r1 + be1 * vecs[0]
        s1 = w1 + be1 * vecs[1]
        z1 = n1 + be1 * vecs[2]
        out_ref[0] = al0 * vecs[0] + al1 * p1
        r2 = r1 - al1 * s1
        w2 = w1 - al1 * z1
        for i, value in enumerate((p1, s1, z1, r2, w2, n1 - al1 * (be1 * vecs[3]))):
            kept[i] = value
        for i, (a, b) in enumerate(
            ((r2, r2), (r2, w2), (w2, w2), (r2, s1), (w2, s1), (s1, s1), (r2, z1), (w2, z1), (s1, z1))
        ):
            part_sums[i : i + 1, :] = row_sums(a, b)

    def operate(k):
        @pl.loop(0, LEVELS)
        def _(i):
            li = LEVELS - 1 - i
            m = level_index(li)

            @pl.loop(0, HALF // 32)
            def _(h):
                found = [upad[pl.ds(rows[m, 0, h * 32 + j] + 8, 1), :] for j in range(32)]
                for j in range(32):
                    send[k, li, pl.ds(h * 32 + j, 1), :] = found[j]

            level_copy(k, li).start()

        csend[k, 0] = upad[7 + NB : 8 + NB, :]
        csend[k, 1] = upad[8:9, :]
        cycle_copy(k, 0).start()
        cycle_copy(k, 1).start()

        @pl.when(k == 0)
        def _():
            convert()

        @pl.when(k >= 2)
        def _():
            reduce_middle(k - 2)

        @pl.when((k == 1) | (k == 2))
        def _():
            vec = vecs[k - 1]
            put_sums(k - 1, [row_sums(vec, vec), row_sums(vec, vecs[k])])
            reduce_begin(k - 1)

        def local(t, carry):
            for part in range(8):
                g = pl.multiple_of(t * 64 + part * 8, 8)
                here = upad[pl.ds(g + 8, 8), :]
                before = upad[pl.ds(g + 7, 8), :]
                own = products(here * wv[pl.ds(g, 8), :], [dids[g + j] for j in range(8)])
                acc_ref[pl.ds(g, 8), :] = shift_ref[pl.ds(g, 8), :] * here + own
                edge = (here - before) * wv[pl.ds(EDGE0 + g, 8), :]
                f_ref[pl.ds(g, 8), :] = products(edge, [cids[0, g + j] for j in range(8)])
            return carry

        lax.fori_loop(0, 2, local, 0)

        def level(li):
            m = level_index(li)
            for h in range(8):
                c = pl.multiple_of(li * HALF + h * 8, 8)
                diff = send[k, li, h * 8 : h * 8 + 8, :] - recv[k, li, h * 8 : h * 8 + 8, :]
                out = products(diff * wv[pl.ds(LINK0 + c, 8), :], [lids[m, 0, h * 8 + j] for j in range(8)])
                high = out.astype(BF16).astype(F32)
                ol_ref[pl.ds(c, 8), 0:BS] = high
                ol_ref[pl.ds(c, 8), BS:] = out - high

        def two_levels(i, carry):
            level_copy(k, 2 * i).wait_recv()
            level_copy(k, 2 * i + 1).wait_recv()
            level(2 * i)
            level(2 * i + 1)
            return carry

        lax.fori_loop(0, LEVELS // 2, two_levels, 0)

        @pl.when(k == 2)
        def _():
            total = reduce_end(0)
            scal[0] = lane(total, 0)
            scal[1] = lane(total, 1)

        @pl.when(k == 3)
        def _():
            prepare()

        level_copy(k, LEVELS - 1).wait_recv()
        level(LEVELS - 1)
        cycle_copy(k, 0).wait()
        cycle_copy(k, 1).wait()
        sub8 = lax.broadcasted_iota(jnp.int32, (8, BS), 0)
        edge = jnp.where(sub8 == 0, upad[8:9, :] - crecv[k, 0], crecv[k, 1] - upad[7 + NB : 8 + NB, :])
        bound = products(edge * bw[...], [cids[0, 0], cids[1, NB - 1]])
        f_ref[0:1, :] = bound[0:1, :]
        f_ref[NB : NB + 1, :] = bound[1:2, :]
        spread = jnp.dot(st[...], ol_ref[...].astype(BF16), preferred_element_type=F32)
        acc_ref[...] = acc_ref[...] + (f_ref[0:NB, :] - f_ref[1 : NB + 1, :]) + (spread[:, :BS] + spread[:, BS:])

        for li in range(LEVELS):
            level_copy(k, li).wait_send()

    vecs[0] = upad[8 : 8 + NB, :]

    def iteration(k, carry):
        operate(k)
        vecs[k + 1] = acc_ref[...]

        @pl.when(k < 2)
        def _():
            upad[8 : 8 + NB, :] = acc_ref[...]

        @pl.when(k == 2)
        def _():
            upad[8 : 8 + NB, :] = vecs[2] - wide(scal[0] / scal[1]) * vecs[3]

        return carry

    lax.fori_loop(0, ITERS, iteration, 0)
    norm1, alpha1 = scal[2], scal[3]
    n2 = kept[5] - wide(alpha1) * acc_ref[...]
    kept[5] = n2
    late = [row_sums(kept[3], n2), row_sums(kept[4], n2), row_sums(kept[1], n2)]
    put_sums(2, [part_sums[i : i + 1, :] for i in range(9)] + late)
    reduce_begin(2)
    reduce_middle(2)
    total = reduce_end(2)
    rr, rw, ww, rs, ws, ss, rz, wz, sz, rn, wn, sn = (lane(total, i) for i in range(12))
    beta2 = rr / norm1
    alpha2 = rr / (rw - beta2 * rr / alpha1)
    c, d = alpha2, alpha2 * beta2
    norm3 = rr + c * c * ww + d * d * ss - 2.0 * (c * rw + d * rs - c * d * ws)
    product3 = rw - c * (rn + ww) - d * (rz + ws) + c * c * wn + c * d * (wz + sn) + d * d * sz
    beta3 = norm3 / rr
    alpha3 = norm3 / (product3 - beta3 * norm3 / alpha2)
    al2, be2, al3, be3 = wide(alpha2), wide(beta2), wide(alpha3), wide(beta3)
    p2 = kept[3] + be2 * kept[0]
    s2 = kept[4] + be2 * kept[1]
    r3 = kept[3] - al2 * s2
    w3 = kept[4] - al2 * (kept[5] + be2 * kept[2])
    out_ref[0] = out_ref[0] + al2 * p2 + al3 * (r3 + be3 * p2)
    out_ref[1] = r3 - al3 * (w3 + be3 * s2)


def per_device(
    right_side,
    diag_shift,
    dictionary,
    diag_ids,
    diag_gain,
    cycle_ids,
    cycle_weights,
    link_rows,
    link_ids,
    link_weights,
):

    vec = (NB, BS)
    across = (1, 0, 2)
    vmem = pl.BlockSpec(memory_space=pltpu.VMEM)
    args = (
        right_side.reshape(vec), diag_shift.reshape(vec), dictionary, diag_ids, diag_gain.reshape(1, NB),
        cycle_ids.T, cycle_weights.T, jnp.transpose(link_rows, across), jnp.transpose(link_ids, across),
        jnp.transpose(link_weights, across),
    )
    out = pl.pallas_call(
        kernel,
        out_shape=jax.ShapeDtypeStruct((2, *vec), F32),
        in_specs=[pl.BlockSpec(memory_space=pl.ANY)] * len(args),
        out_specs=vmem,
        scratch_shapes=[
            pltpu.VMEM((BS, BS, 2 * BS), BF16),
            pltpu.VMEM((BS, BS, BS), F32),
            pltpu.VMEM(vec, F32),
            pltpu.SMEM((NB,), jnp.int32),
            pltpu.SMEM((2, NB), jnp.int32),
            pltpu.SMEM((LEVELS, 1, HALF), jnp.int32),
            pltpu.SMEM((LEVELS, 1, HALF), jnp.int32),
            pltpu.VMEM((1, NB), F32),
            pltpu.VMEM((2, NB), F32),
            pltpu.VMEM((LEVELS, 1, HALF), jnp.int32),
            pltpu.VMEM((LEVELS, 1, HALF), F32),
            pltpu.VMEM((LINK0 + 3 * NB, BS), F32),
            pltpu.VMEM((8, BS), F32),
            pltpu.VMEM((NB, 3 * BS), BF16),
            pltpu.VMEM((NB + 8, BS), F32),
            pltpu.VMEM((ITERS + 1, NB, BS), F32),
            pltpu.VMEM(vec, F32),
            pltpu.VMEM((NB + 8, BS), F32),
            pltpu.VMEM((3 * BS, 2 * BS), F32),
            pltpu.VMEM((4, 8, BS), F32),
            pltpu.VMEM((6, NB, BS), F32),
            pltpu.VMEM((16, BS), F32),
            pltpu.VMEM((ITERS, LEVELS, HALF, BS), F32),
            pltpu.VMEM((ITERS, LEVELS, HALF, BS), F32),
            pltpu.VMEM((ITERS, 2, 1, BS), F32),
            pltpu.VMEM((ITERS, 2, 1, BS), F32),
            pltpu.VMEM((SUMS, 1, BS), F32),
            pltpu.VMEM((SUMS, PARTS, 1, BS), F32),
            pltpu.VMEM((SUMS, 1, BS), F32),
            pltpu.VMEM((SUMS, PARTS, 1, BS), F32),
            pltpu.SemaphoreType.DMA((len(args),)),
            pltpu.SemaphoreType.DMA((16,)),
            pltpu.SemaphoreType.DMA((ITERS, LEVELS)),
            pltpu.SemaphoreType.DMA((ITERS, LEVELS)),
            pltpu.SemaphoreType.DMA((ITERS, 2)),
            pltpu.SemaphoreType.DMA((ITERS, 2)),
            pltpu.SemaphoreType.DMA((SUMS, PARTS)),
            pltpu.SemaphoreType.DMA((SUMS, PARTS)),
            pltpu.SemaphoreType.DMA((SUMS, PARTS)),
            pltpu.SemaphoreType.DMA((SUMS, PARTS)),
        ],
        compiler_params=pltpu.CompilerParams(
            collective_id=0, has_side_effects=True, vmem_limit_bytes=58 * 1024 * 1024
        ),
        name="cg",
    )(*args)
    return out[0].reshape(-1), out[1].reshape(-1)


def solution(mesh):
    placed = (
        P(AXIS),
        P(AXIS),
        P(),
        P(AXIS),
        P(AXIS),
        P(AXIS, None),
        P(AXIS, None),
        P(AXIS, None, None),
        P(AXIS, None, None),
        P(AXIS, None, None),
    )
    return jax.shard_map(
        per_device, mesh=mesh, in_specs=placed, out_specs=(P(AXIS), P(AXIS)), check_vma=False
    )
```

```python
import functools

import jax
import jax.numpy as jnp
from jax import lax
from jax.experimental import pallas as pl
from jax.experimental.pallas import tpu as pltpu
from jax.sharding import PartitionSpec as P

AXIS = "rows"
MESH = pl.DeviceIdType.MESH
ITERS = 4
BS = 128
NB = 128
HALF = 64
LEVELS = 5
LINKS = LEVELS * HALF
EDGE0 = NB
LINK0 = 2 * NB
SUMS = 3
PARTS = 16
F32 = jnp.float32
BF16 = jnp.bfloat16


def level_mask(li):
    q = li // 2
    return 8 * (1 + q + q // 2) * (1 + 7 * (li % 2))


def level_index(li):
    return 4 - li // 2 - 3 * (li % 2)


def level_partner(me, li):
    mask = level_mask(li)
    return me + mask - 2 * mask * ((me // mask) % 2)


def split_rows(d):
    high = d.astype(BF16).astype(F32)
    return jnp.concatenate([high, d - high], axis=0).astype(BF16)


def kernel(
    b_hbm, shift_hbm, dict_hbm, dids_hbm, gain_hbm, cids_hbm, cw_hbm, lrow_hbm, lids_hbm, lw_hbm,
    out_ref,
    g_ref, stage, shift_ref, dids, cids, rows, lids, gain, cw, lrow, lw,
    wv, bw, st, upad, vecs, acc_ref, f_ref, ol_ref, scal, kept, part_sums,
    send, recv, csend, crecv, ar_src, ar_one, ar_mid, ar_two,
    in_sem, dict_sem, lv_s, lv_r, cy_s, cy_r, a1_s, a1_r, a2_s, a2_r,
):
    me = lax.axis_index(AXIS)
    n = lax.axis_size(AXIS)
    core, xs, zs, ys = me % 2, (me // 2) % 4, (me // 8) % 8, me // 64
    nxt, prv = (me + 1) % n, (me + n - 1) % n

    def one_peer(j):
        return ys * 64 + ((zs + j // 2) % 8) * 8 + xs * 2 + (core + j % 2) % 2

    def two_peer(j):
        return ((ys + j // 4) % 4) * 64 + zs * 8 + ((xs + j % 4) % 4) * 2 + core

    small = [
        pltpu.make_async_copy(src, dst, in_sem.at[i])
        for i, (src, dst) in enumerate((
            (b_hbm, upad.at[pl.ds(8, NB)]), (lrow_hbm, rows), (lrow_hbm, lrow), (shift_hbm, shift_ref),
            (gain_hbm, gain), (cw_hbm, cw), (lw_hbm, lw), (dids_hbm, dids), (cids_hbm, cids), (lids_hbm, lids),
        ))
    ]
    for copy in small:
        copy.start()

    def dict_copy(c):
        part = pl.ds(c * 8, 8)
        return pltpu.make_async_copy(dict_hbm.at[part], stage.at[part], dict_sem.at[c])

    @pl.loop(0, 16)
    def _(c):
        dict_copy(c).start()

    barrier = pltpu.get_barrier_semaphore()

    @pl.loop(1, PARTS)
    def _(j):
        pl.semaphore_signal(barrier, inc=1, device_id={AXIS: one_peer(j)}, device_id_type=MESH)
        pl.semaphore_signal(barrier, inc=1, device_id={AXIS: two_peer(j)}, device_id_type=MESH)

    pl.semaphore_signal(barrier, inc=1, device_id={AXIS: nxt}, device_id_type=MESH)
    pl.semaphore_signal(barrier, inc=1, device_id={AXIS: prv}, device_id_type=MESH)

    for copy in small:
        copy.wait()

    eye = lax.broadcasted_iota(jnp.int32, (NB, BS), 0) == lax.broadcasted_iota(jnp.int32, (NB, BS), 1)
    row_of = lax.broadcasted_iota(jnp.int32, (NB, BS), 0)

    def spread_rows(row):
        return jnp.broadcast_to(jnp.sum(jnp.where(eye, row, 0.0), axis=1, keepdims=True), (NB, BS))

    wv[0:NB, :] = spread_rows(gain[...])
    wv[EDGE0 : EDGE0 + NB, :] = spread_rows(cw[0:1, :])
    for blk in range(3):
        m0, m1 = level_index(2 * blk), level_index(min(2 * blk + 1, LEVELS - 1))
        lanes = slice(blk * BS, (blk + 1) * BS)
        wv[LINK0 + blk * NB : LINK0 + (blk + 1) * NB, :] = spread_rows(jnp.concatenate([lw[m0], lw[m1]], axis=1))
        second = lrow[m1] if blk < 2 else jnp.full((1, HALF), -1, jnp.int32)
        hit = row_of == jnp.concatenate([lrow[m0], second], axis=1)
        st[:, lanes] = jnp.where(hit, 1.0, 0.0).astype(BF16)
    bw[0:1, :] = wv[EDGE0 : EDGE0 + 1, :]
    bw[1:8, :] = jnp.broadcast_to(cw[1:2, BS - 1 :], (7, BS))
    upad[0:8, :] = jnp.zeros((8, BS), F32)
    ol_ref[LINKS:, :] = jnp.zeros((64, 2 * BS), F32)
    pl.semaphore_wait(barrier, 2 * (PARTS - 1) + 2)

    sub16 = lax.broadcasted_iota(jnp.int32, (16, BS), 0) % 8

    def products(d, picks):
        lhs = split_rows(d)
        out = jnp.zeros((16, 2 * BS), F32)
        for j, pick in enumerate(picks):
            picked = jnp.where(sub16 == j, lhs, jnp.zeros_like(lhs))
            out = out + jnp.dot(picked, g_ref[pick], preferred_element_type=F32)
        return (out[:8, :BS] + out[8:, BS:]) + (out[:8, BS:] + out[8:, :BS])

    def level_copy(k, li):
        return pltpu.make_async_remote_copy(
            src_ref=send.at[k, li], dst_ref=recv.at[k, li], send_sem=lv_s.at[k, li], recv_sem=lv_r.at[k, li],
            device_id={AXIS: level_partner(me, li)}, device_id_type=MESH)

    def cycle_copy(k, side):
        return pltpu.make_async_remote_copy(
            src_ref=csend.at[k, side], dst_ref=crecv.at[k, side], send_sem=cy_s.at[k, side],
            recv_sem=cy_r.at[k, side], device_id={AXIS: nxt if side == 0 else prv}, device_id_type=MESH)

    def one_copy(k, j):
        return pltpu.make_async_remote_copy(
            src_ref=ar_src.at[k], dst_ref=ar_one.at[k, j], send_sem=a1_s.at[k, j], recv_sem=a1_r.at[k, j],
            device_id={AXIS: one_peer(j)}, device_id_type=MESH)

    def two_copy(k, j):
        return pltpu.make_async_remote_copy(
            src_ref=ar_mid.at[k], dst_ref=ar_two.at[k, j], send_sem=a2_s.at[k, j], recv_sem=a2_r.at[k, j],
            device_id={AXIS: two_peer(j)}, device_id_type=MESH)

    def reduce_begin(k):
        for j in sorted(range(1, PARTS), key=lambda j: abs(j // 2 - 4)):
            one_copy(k, j).start()

    def reduce_middle(k):
        for j in range(1, PARTS):
            one_copy(k, j).wait_recv()
        ar_one[k, 0] = ar_src[k]
        ar_mid[k] = jnp.sum(ar_one[k], axis=0)

        for j in sorted(range(1, PARTS), key=lambda j: abs(j // 4 - 2) + abs(j % 4 - 2)):
            two_copy(k, j).start()
        for j in range(1, PARTS):
            one_copy(k, j).wait_send()

    def reduce_end(k):
        for j in range(1, PARTS):
            two_copy(k, j).wait()
        ar_two[k, 0] = ar_mid[k]
        return jnp.sum(ar_two[k], axis=0)

    def row_sums(a, b):
        return jnp.sum(a * b, axis=0, keepdims=True)

    def put_sums(k, parts):
        count = -(-len(parts) // 8) * 8
        parts = parts + [jnp.zeros((1, BS), F32)] * (count - len(parts))
        sums = jnp.sum(jnp.concatenate(parts, axis=0), axis=1, keepdims=True)
        shape = (count, BS)
        own = lax.broadcasted_iota(jnp.int32, shape, 0) == lax.broadcasted_iota(jnp.int32, shape, 1)
        ar_src[k] = jnp.sum(jnp.where(own, jnp.broadcast_to(sums, shape), 0.0), axis=0, keepdims=True)

    def lane(total, i):
        return jnp.broadcast_to(total[:, i : i + 1], (8, BS))

    def wide(value):
        return jnp.tile(value, (NB // 8, 1))

    def convert():
        @pl.loop(0, 16)
        def _(c):
            dict_copy(c).wait()

            @pl.loop(0, 2)
            def _(i):
                for j in range(4):
                    at = c * 8 + i * 4 + j
                    block = stage[at]
                    high = block.astype(BF16)
                    g_ref[at, :, 0:BS] = high
                    g_ref[at, :, BS:] = (block - high.astype(F32)).astype(BF16)

    def prepare():
        total = reduce_end(1)
        m0, m1, m2, m3 = scal[0], scal[1], lane(total, 0), lane(total, 1)
        alpha0 = m0 / m1
        norm1 = m0 - 2.0 * alpha0 * m1 + alpha0 * alpha0 * m2
        product1 = m1 - 2.0 * alpha0 * m2 + alpha0 * alpha0 * m3
        beta1 = norm1 / m0
        alpha1 = norm1 / (product1 - beta1 * norm1 / alpha0)
        scal[2] = norm1
        scal[3] = alpha1
        al0, al1, be1 = wide(alpha0), wide(alpha1), wide(beta1)
        r1 = vecs[0] - al0 * vecs[1]
        w1 = vecs[1] - al0 * vecs[2]
        n1 = upad[8 : 8 + NB, :]
        p1 = r1 + be1 * vecs[0]
        s1 = w1 + be1 * vecs[1]
        z1 = n1 + be1 * vecs[2]
        out_ref[0] = al0 * vecs[0] + al1 * p1
        r2 = r1 - al1 * s1
        w2 = w1 - al1 * z1
        for i, value in enumerate((p1, s1, z1, r2, w2, n1 - al1 * (be1 * vecs[3]))):
            kept[i] = value
        for i, (a, b) in enumerate(
            ((r2, r2), (r2, w2), (w2, w2), (r2, s1), (w2, s1), (s1, s1), (r2, z1), (w2, z1), (s1, z1))
        ):
            part_sums[i : i + 1, :] = row_sums(a, b)

    def operate(k):
        for li in reversed(range(LEVELS)):
            m = level_index(li)
            for h in range(HALF // 32):
                found = [upad[pl.ds(rows[m, 0, h * 32 + j] + 8, 1), :] for j in range(32)]
                for j in range(32):
                    send[k, li, pl.ds(h * 32 + j, 1), :] = found[j]

            level_copy(k, li).start()

        csend[k, 0] = upad[7 + NB : 8 + NB, :]
        csend[k, 1] = upad[8:9, :]
        cycle_copy(k, 0).start()
        cycle_copy(k, 1).start()

        @pl.when(k == 0)
        def _():
            convert()

        @pl.when(k >= 2)
        def _():
            reduce_middle(k - 2)

        @pl.when((k == 1) | (k == 2))
        def _():
            vec = vecs[k - 1]
            put_sums(k - 1, [row_sums(vec, vec), row_sums(vec, vecs[k])])
            reduce_begin(k - 1)

        def local(t, carry):
            for part in range(8):
                g = pl.multiple_of(t * 64 + part * 8, 8)
                here = upad[pl.ds(g + 8, 8), :]
                before = upad[pl.ds(g + 7, 8), :]
                own = products(here * wv[pl.ds(g, 8), :], [dids[g + j] for j in range(8)])
                acc_ref[pl.ds(g, 8), :] = shift_ref[pl.ds(g, 8), :] * here + own
                edge = (here - before) * wv[pl.ds(EDGE0 + g, 8), :]
                f_ref[pl.ds(g, 8), :] = products(edge, [cids[0, g + j] for j in range(8)])
            return carry

        lax.fori_loop(0, 2, local, 0)

        def level(li):
            m = level_index(li)
            for h in range(8):
                c = pl.multiple_of(li * HALF + h * 8, 8)
                diff = send[k, li, h * 8 : h * 8 + 8, :] - recv[k, li, h * 8 : h * 8 + 8, :]
                out = products(diff * wv[pl.ds(LINK0 + c, 8), :], [lids[m, 0, h * 8 + j] for j in range(8)])
                high = out.astype(BF16).astype(F32)
                ol_ref[pl.ds(c, 8), 0:BS] = high
                ol_ref[pl.ds(c, 8), BS:] = out - high

        def two_levels(i, carry):
            level_copy(k, 2 * i).wait_recv()
            level_copy(k, 2 * i + 1).wait_recv()
            level(2 * i)
            level(2 * i + 1)
            return carry

        lax.fori_loop(0, LEVELS // 2, two_levels, 0)

        @pl.when(k == 2)
        def _():
            total = reduce_end(0)
            scal[0] = lane(total, 0)
            scal[1] = lane(total, 1)

        @pl.when(k == 3)
        def _():
            prepare()

        level_copy(k, LEVELS - 1).wait_recv()
        level(LEVELS - 1)
        cycle_copy(k, 0).wait()
        cycle_copy(k, 1).wait()
        sub8 = lax.broadcasted_iota(jnp.int32, (8, BS), 0)
        edge = jnp.where(sub8 == 0, upad[8:9, :] - crecv[k, 0], crecv[k, 1] - upad[7 + NB : 8 + NB, :])
        bound = products(edge * bw[...], [cids[0, 0], cids[1, NB - 1]])
        f_ref[0:1, :] = bound[0:1, :]
        f_ref[NB : NB + 1, :] = bound[1:2, :]
        spread = jnp.dot(st[...], ol_ref[...].astype(BF16), preferred_element_type=F32)
        acc_ref[...] = acc_ref[...] + (f_ref[0:NB, :] - f_ref[1 : NB + 1, :]) + (spread[:, :BS] + spread[:, BS:])

        for li in range(LEVELS):
            level_copy(k, li).wait_send()

    vecs[0] = upad[8 : 8 + NB, :]

    def iteration(k, carry):
        operate(k)
        vecs[k + 1] = acc_ref[...]

        @pl.when(k < 2)
        def _():
            upad[8 : 8 + NB, :] = acc_ref[...]

        @pl.when(k == 2)
        def _():
            upad[8 : 8 + NB, :] = vecs[2] - wide(scal[0] / scal[1]) * vecs[3]

        return carry

    lax.fori_loop(0, ITERS, iteration, 0)
    norm1, alpha1 = scal[2], scal[3]
    n2 = kept[5] - wide(alpha1) * acc_ref[...]
    kept[5] = n2
    late = [row_sums(kept[3], n2), row_sums(kept[4], n2), row_sums(kept[1], n2)]
    put_sums(2, [part_sums[i : i + 1, :] for i in range(9)] + late)
    reduce_begin(2)
    reduce_middle(2)
    total = reduce_end(2)
    rr, rw, ww, rs, ws, ss, rz, wz, sz, rn, wn, sn = (lane(total, i) for i in range(12))
    beta2 = rr / norm1
    alpha2 = rr / (rw - beta2 * rr / alpha1)
    c, d = alpha2, alpha2 * beta2
    norm3 = rr + c * c * ww + d * d * ss - 2.0 * (c * rw + d * rs - c * d * ws)
    product3 = rw - c * (rn + ww) - d * (rz + ws) + c * c * wn + c * d * (wz + sn) + d * d * sz
    beta3 = norm3 / rr
    alpha3 = norm3 / (product3 - beta3 * norm3 / alpha2)
    al2, be2, al3, be3 = wide(alpha2), wide(beta2), wide(alpha3), wide(beta3)
    p2 = kept[3] + be2 * kept[0]
    s2 = kept[4] + be2 * kept[1]
    r3 = kept[3] - al2 * s2
    w3 = kept[4] - al2 * (kept[5] + be2 * kept[2])
    out_ref[0] = out_ref[0] + al2 * p2 + al3 * (r3 + be3 * p2)
    out_ref[1] = r3 - al3 * (w3 + be3 * s2)


def per_device(
    right_side,
    diag_shift,
    dictionary,
    diag_ids,
    diag_gain,
    cycle_ids,
    cycle_weights,
    link_rows,
    link_ids,
    link_weights,
):

    vec = (NB, BS)
    across = (1, 0, 2)
    vmem = pl.BlockSpec(memory_space=pltpu.VMEM)
    args = (
        right_side.reshape(vec), diag_shift.reshape(vec), dictionary, diag_ids, diag_gain.reshape(1, NB),
        cycle_ids.T, cycle_weights.T, jnp.transpose(link_rows, across), jnp.transpose(link_ids, across),
        jnp.transpose(link_weights, across),
    )
    out = pl.pallas_call(
        kernel,
        out_shape=jax.ShapeDtypeStruct((2, *vec), F32),
        in_specs=[pl.BlockSpec(memory_space=pl.ANY)] * len(args),
        out_specs=vmem,
        scratch_shapes=[
            pltpu.VMEM((BS, BS, 2 * BS), BF16),
            pltpu.VMEM((BS, BS, BS), F32),
            pltpu.VMEM(vec, F32),
            pltpu.SMEM((NB,), jnp.int32),
            pltpu.SMEM((2, NB), jnp.int32),
            pltpu.SMEM((LEVELS, 1, HALF), jnp.int32),
            pltpu.SMEM((LEVELS, 1, HALF), jnp.int32),
            pltpu.VMEM((1, NB), F32),
            pltpu.VMEM((2, NB), F32),
            pltpu.VMEM((LEVELS, 1, HALF), jnp.int32),
            pltpu.VMEM((LEVELS, 1, HALF), F32),
            pltpu.VMEM((LINK0 + 3 * NB, BS), F32),
            pltpu.VMEM((8, BS), F32),
            pltpu.VMEM((NB, 3 * BS), BF16),
            pltpu.VMEM((NB + 8, BS), F32),
            pltpu.VMEM((ITERS + 1, NB, BS), F32),
            pltpu.VMEM(vec, F32),
            pltpu.VMEM((NB + 8, BS), F32),
            pltpu.VMEM((3 * BS, 2 * BS), F32),
            pltpu.VMEM((4, 8, BS), F32),
            pltpu.VMEM((6, NB, BS), F32),
            pltpu.VMEM((16, BS), F32),
            pltpu.VMEM((ITERS, LEVELS, HALF, BS), F32),
            pltpu.VMEM((ITERS, LEVELS, HALF, BS), F32),
            pltpu.VMEM((ITERS, 2, 1, BS), F32),
            pltpu.VMEM((ITERS, 2, 1, BS), F32),
            pltpu.VMEM((SUMS, 1, BS), F32),
            pltpu.VMEM((SUMS, PARTS, 1, BS), F32),
            pltpu.VMEM((SUMS, 1, BS), F32),
            pltpu.VMEM((SUMS, PARTS, 1, BS), F32),
            pltpu.SemaphoreType.DMA((len(args),)),
            pltpu.SemaphoreType.DMA((16,)),
            pltpu.SemaphoreType.DMA((ITERS, LEVELS)),
            pltpu.SemaphoreType.DMA((ITERS, LEVELS)),
            pltpu.SemaphoreType.DMA((ITERS, 2)),
            pltpu.SemaphoreType.DMA((ITERS, 2)),
            pltpu.SemaphoreType.DMA((SUMS, PARTS)),
            pltpu.SemaphoreType.DMA((SUMS, PARTS)),
            pltpu.SemaphoreType.DMA((SUMS, PARTS)),
            pltpu.SemaphoreType.DMA((SUMS, PARTS)),
        ],
        compiler_params=pltpu.CompilerParams(
            collective_id=0, has_side_effects=True, vmem_limit_bytes=58 * 1024 * 1024
        ),
        name="cg",
    )(*args)
    return out[0].reshape(-1), out[1].reshape(-1)


def solution(mesh):
    placed = (
        P(AXIS),
        P(AXIS),
        P(),
        P(AXIS),
        P(AXIS),
        P(AXIS, None),
        P(AXIS, None),
        P(AXIS, None, None),
        P(AXIS, None, None),
        P(AXIS, None, None),
    )
    return jax.shard_map(
        per_device, mesh=mesh, in_specs=placed, out_specs=(P(AXIS), P(AXIS)), check_vma=False
    )
```
